32 devices in a mesh: bx: 4 (over x, core), by: 8 (over z, y).
Axes of the slice: x: 2, y: 2, z: 4, core: 2. Of those that a mesh axis runs over, the one named last changes fastest.
Arguments:
- atom_pos: float32 [3, 16, 64, 128], P(None, 'bx', 'by'), may hold values from 0 to 1
- b_factor: float32 [16, 64, 128], P('bx', 'by'), may hold values from 100 to 400
- amplitude: float32 [16, 64, 128], P('bx', 'by'), may hold values from 0.5 to 2
- counts: int32 [16, 64], P('bx', 'by'), may hold values from 1 to 128, as said below
- density_map: bfloat16 [256, 1024, 128], P('bx', 'by'), may hold values from -1 to 1
Outputs:
- residual_map: bfloat16 [256, 1024, 128], P('bx', 'by')
- atom_gradient: float32 [4, 16, 64, 128], P(None, 'bx', 'by')
The draws below stay inside these ranges and needn't reach their ends.
Inputs may be any that keep to these rules, and one draw needn't show every extreme that they name: Slots below counts[a, b] of subbrick (a, b) hold its atoms, the others are padding; in every draw some subbrick is full.
All inputs are finite; a program needn't handle non-finite values.
Results may differ from the reference program's by a relative error of at most 0.001.
Values sent between devices are 32-bit elements; how exact they have to be, the bound alone decides.
No kernel may reach another device: no remote copies, remote signals or barrier semaphores. Data moves between devices by JAX's collectives and lax.ppermute only.
A program may use at most 128 MiB of HBM per device.

```python
import math
import jax
import jax.numpy as jnp
from jax import lax

SUB = 16
RAD = 4
TILE = 24
CAP = 128
DEPTH = 128
NSX = 16
NSY = 64
NX = 256
NY = 1024


def draw_counts(key, part):
    key_level, key_count, key_full = jax.random.split(key, 3)
    density_level = jax.random.randint(key_level, (NSX, NSY), 1, 5)
    upper_bound = CAP // 4 * density_level
    lower_bound = jnp.maximum(upper_bound // 2, 1)
    drawn_counts = jax.random.randint(key_count, (NSX, NSY), lower_bound, upper_bound + 1)
    full_spot = jax.random.randint(key_full, (), 0, NSX * NSY)
    flat_counts = drawn_counts.reshape(-1).at[full_spot].set(CAP)
    return flat_counts.reshape(NSX, NSY).astype(jnp.int32)


def draw_atom_pos(key, part):
    key_snap, key_side, key_pos = jax.random.split(key, 3)
    shape = (3, NSX, NSY, CAP)
    inside = jax.random.uniform(key_pos, shape, jnp.float32)
    snapped = jax.random.randint(key_snap, shape, 0, 5) < 2
    side = jax.random.randint(key_side, shape, 0, 2).astype(jnp.float32)
    edge = side
    planar = jnp.arange(3)[:, None, None, None] < 2
    return jnp.where(snapped & planar, edge, inside).astype(jnp.float32)


def draw_density_map(key, part):
    spread_scale = 3.0 * math.sqrt(CAP / (SUB * SUB * DEPTH))
    shape = (NX, NY, DEPTH)
    values = jnp.clip(jax.random.normal(key, shape, jnp.float32), -4.0, 4.0)
    return (spread_scale * values).astype(jnp.bfloat16)


def block_levels(key, shape, shards, least, high):
    level, own = 1.0, jax.random.fold_in(key, 6)
    for position, shards_of in shards:
        heights = jnp.exp(jax.random.uniform(jax.random.fold_in(own, position), (shards_of,), jnp.float32, least / len(shards), high / len(shards)))
        level = level * jnp.repeat(heights, shape[position] // shards_of).reshape([-1 if axis == position else 1 for axis in range(len(shape))])
    return level


def setup_inputs(seed: int = 0) -> dict:
    seeds = jax.random.split(jax.random.key(seed), 6)
    atom_pos = draw_atom_pos(jax.random.fold_in(seeds[5], 71), 0)
    b_factor = jnp.clip(jnp.exp(math.log(400.0) - 1.3862944 * jax.random.uniform(seeds[1], (NSX, NSY, CAP), jnp.float32) ** block_levels(seeds[1], (NSX, NSY, CAP), ((0, 4), (1, 8)), -0.2, 0.2)), 100.0, 400.0)
    amplitude = jnp.clip(jnp.exp(math.log(2.0) - 1.3862944 * jax.random.uniform(seeds[2], (NSX, NSY, CAP), jnp.float32) ** block_levels(seeds[2], (NSX, NSY, CAP), ((0, 4), (1, 8)), -0.2, 0.2)), 0.5, 2.0)
    counts = draw_counts(jax.random.fold_in(seeds[5], 71), 0)
    density_map = draw_density_map(jax.random.fold_in(seeds[5], 71), 0)
    return dict(atom_pos=atom_pos, b_factor=b_factor, amplitude=amplitude, counts=counts, density_map=density_map)


EIGHT_PI_SQ = 8.0 * math.pi ** 2
BLUR_VAR = 0.5

def profiles(coordinate, sharpness, span_len, offset):
    grid_pos = (jnp.arange(span_len) + offset).astype(jnp.float32)
    distance = grid_pos - coordinate[..., None]
    square = distance * distance
    reach_sq = float(RAD * RAD)
    falloff = jnp.where(square < reach_sq, 1.0 - square / reach_sq, 0.0)
    exponent = jnp.exp(-sharpness[..., None] * square)
    profile = exponent * falloff * falloff
    slope_d = 2.0 * distance * exponent * falloff * (sharpness[..., None] * falloff + 2.0 / reach_sq)
    width_d = -square * profile
    return (profile, slope_d, width_d)

def all_profiles(coords, sharpness):
    along_x = profiles(coords[0], sharpness, TILE, -RAD)
    along_y = profiles(coords[1], sharpness, TILE, -RAD)
    along_z = profiles(coords[2], sharpness, DEPTH, 0)
    return (along_x, along_y, along_z)

def atom_terms(atom_pos, b_factor, amplitude, counts):
    live_slot = jnp.arange(amplitude.shape[-1])[None, None, :] < counts[..., None]
    weight = jnp.where(live_slot, amplitude, 0.0)
    sharpness = 0.5 / (b_factor / EIGHT_PI_SQ + BLUR_VAR)
    coords = jnp.stack([SUB * atom_pos[0], SUB * atom_pos[1], DEPTH * atom_pos[2]])
    return (weight, sharpness, coords)

def render(value_x, value_y, value_z, weight):
    plane_xy = value_x[..., :, None] * value_y[..., None, :]
    plane_xy = plane_xy.reshape(plane_xy.shape[:-2] + (TILE * TILE,))
    return jnp.einsum('...cm,...ck->...mk', plane_xy, value_z * weight[..., None], precision=lax.Precision.HIGHEST)

def spread(tile_set, axis_dim):
    tile_count = tile_set.shape[axis_dim]
    head_part = lax.slice_in_dim(tile_set, 0, SUB, axis=axis_dim + 1)
    tail_part = lax.slice_in_dim(tile_set, SUB, TILE, axis=axis_dim + 1)
    tail_pad = [(0, 0)] * tile_set.ndim
    tail_pad[axis_dim + 1] = (0, SUB - 2 * RAD)
    tail_part = jnp.pad(tail_part, tail_pad)
    new_shape = tile_set.shape[:axis_dim] + (tile_count * SUB,) + tile_set.shape[axis_dim + 2:]
    head_part = head_part.reshape(new_shape)
    tail_part = tail_part.reshape(new_shape)
    pad_after = [(0, 0)] * len(new_shape)
    pad_after[axis_dim] = (0, 2 * RAD)
    pad_before = [(0, 0)] * len(new_shape)
    pad_before[axis_dim] = (SUB, 0)
    shifted = lax.slice_in_dim(jnp.pad(tail_part, pad_before), 0, tile_count * SUB + 2 * RAD, axis=axis_dim)
    return jnp.pad(head_part, pad_after) + shifted

def collect(grid_field, axis_dim, tile_count):
    new_shape = grid_field.shape[:axis_dim] + (tile_count, SUB) + grid_field.shape[axis_dim + 1:]
    head_part = lax.slice_in_dim(grid_field, 0, tile_count * SUB, axis=axis_dim).reshape(new_shape)
    pad_after = [(0, 0)] * grid_field.ndim
    pad_after[axis_dim] = (0, SUB - 2 * RAD)
    tail_part = lax.slice_in_dim(jnp.pad(grid_field, pad_after), SUB, tile_count * SUB + SUB, axis=axis_dim).reshape(new_shape)
    tail_part = lax.slice_in_dim(tail_part, 0, 2 * RAD, axis=axis_dim + 1)
    return jnp.concatenate([head_part, tail_part], axis=axis_dim + 1)

def over_y(block_pqc, profile_q):
    return lax.optimization_barrier(jnp.sum(block_pqc * profile_q[..., None, :, :], axis=-2))

def over_x(row_pc, profile_p):
    return lax.optimization_barrier(jnp.sum(row_pc * profile_p, axis=-2))

def gradients(tile_resid, weight, sharpness, along_x, along_y, along_z):
    stacked = jnp.stack(along_z, axis=-3)
    project = jnp.einsum('...mk,...jck->...jmc', tile_resid, stacked, precision=lax.Precision.HIGHEST)
    project = project.reshape(project.shape[:-2] + (TILE, TILE, project.shape[-1]))
    value_x, slope_x, width_x = [jnp.swapaxes(profile, -1, -2) for profile in along_x]
    value_y, slope_y, width_y = [jnp.swapaxes(profile, -1, -2) for profile in along_y]
    base_proj = project[..., 0, :, :, :]
    lift_proj = project[..., 1, :, :, :]
    width_proj = project[..., 2, :, :, :]
    base_value = over_y(base_proj, value_y)
    base_slope = over_y(base_proj, slope_y)
    base_width = over_y(base_proj, width_y)
    lift_value = over_y(lift_proj, value_y)
    width_value = over_y(width_proj, value_y)
    grad_x = weight * over_x(base_value, slope_x)
    grad_y = weight * over_x(base_slope, value_x)
    grad_z = weight * over_x(lift_value, value_x)
    grad_sharp = weight * (over_x(base_value, width_x) + over_x(base_width, value_x) + over_x(width_value, value_x))
    grad_b = grad_sharp * (-2.0 * sharpness * sharpness / EIGHT_PI_SQ)
    return jnp.stack([grad_x, grad_y, grad_z, grad_b], axis=0)

def reference(atom_pos, b_factor, amplitude, counts, density_map):
    weight, sharpness, coords = atom_terms(atom_pos, b_factor, amplitude, counts)
    coords_rows = jnp.moveaxis(coords, 1, 0)
    row_ids = jnp.arange(NSX, dtype=jnp.int32)
    start_field = jnp.zeros((SUB * NSX + 2 * RAD, SUB * NSY + 2 * RAD, DEPTH), jnp.float32)

    def add_row(ext_field, row_item):
        row_index, row_coords, row_sharp, row_weight = row_item
        along_x, along_y, along_z = all_profiles(row_coords, row_sharp)
        rendered = render(along_x[0], along_y[0], along_z[0], row_weight)
        tile_set = jnp.transpose(rendered.reshape(NSY, TILE, TILE, DEPTH), (1, 0, 2, 3))
        strip_row = spread(tile_set, 1)
        row_start = (row_index * SUB).astype(jnp.int32)
        zero_idx = jnp.zeros((), jnp.int32)
        current = lax.dynamic_slice(ext_field, (row_start, zero_idx, zero_idx), strip_row.shape)
        updated = lax.dynamic_update_slice(ext_field, current + strip_row, (row_start, zero_idx, zero_idx))
        return (updated, jnp.zeros((), jnp.float32))
    ext_field = lax.scan(add_row, start_field, (row_ids, coords_rows, sharpness, weight))[0]
    density = ext_field[RAD:RAD + SUB * NSX, RAD:RAD + SUB * NSY]
    residual = density - density_map.astype(jnp.float32)
    padded_resid = jnp.pad(residual, ((RAD, RAD), (RAD, RAD), (0, 0)))

    def row_grad(row_item):
        row_index, row_coords, row_sharp, row_weight = row_item
        along_x, along_y, along_z = all_profiles(row_coords, row_sharp)
        row_start = (row_index * SUB).astype(jnp.int32)
        strip_row = lax.dynamic_slice_in_dim(padded_resid, row_start, TILE, axis=0)
        tile_resid = jnp.transpose(collect(strip_row, 1, NSY), (1, 0, 2, 3)).reshape(NSY, TILE * TILE, DEPTH)
        return gradients(tile_resid, row_weight, row_sharp, along_x, along_y, along_z)
    rows_grad = lax.map(row_grad, (row_ids, coords_rows, sharpness, weight))
    atom_gradient = jnp.moveaxis(rows_grad, 0, 1)
    return (residual.astype(jnp.bfloat16), atom_gradient)
```

```python
import functools
import math

import jax
import jax.numpy as jnp
from jax import lax
from jax.experimental import pallas as pl
from jax.experimental.pallas import tpu as pltpu
from jax.sharding import PartitionSpec as P

SUB = 16
RAD = 4
TILE = 24
CAP = 128
DEPTH = 128
FIELDS = 8

EIGHT_PI_SQ = 8.0 * math.pi**2
BLUR_VAR = 0.5
REACH_SQ = float(RAD * RAD)


def shift(block, axis, step):
    peers = lax.axis_size(axis)
    route = [(i, i + step) for i in range(peers) if 0 <= i + step < peers]
    return lax.ppermute(block, axis, route)


def split(value):
    high = value.astype(jnp.bfloat16)
    low = (value - high.astype(jnp.float32)).astype(jnp.bfloat16)
    return high, low


def base_profile(coordinate, sharpness, span, offset):
    grid = (lax.broadcasted_iota(jnp.int32, (span, CAP), 0) + offset).astype(jnp.float32)
    distance = grid - coordinate
    square = distance * distance
    falloff = jnp.maximum(1.0 - square * (1.0 / REACH_SQ), 0.0)
    damped = jnp.exp(-sharpness * square) * falloff
    return distance, square, falloff, damped


def value_only(coordinate, sharpness, span, offset):
    _, _, falloff, damped = base_profile(coordinate, sharpness, span, offset)
    return damped * falloff


def all_kinds(coordinate, sharpness, span, offset):
    distance, square, falloff, damped = base_profile(coordinate, sharpness, span, offset)
    value = damped * falloff
    slope = 2.0 * distance * (sharpness * value + (2.0 / REACH_SQ) * damped)
    width = -square * value
    return value, slope, width


def kernel(
    rows_n, cols_n,
    valid_ref, atoms_ref, xrim_ref, yrim_ref, map_hbm,
    out_hbm, grad_ref,
    field, pieces, map_v, out_v, prof_x, in_sem, out_sem,
):
    nx, ny = rows_n * SUB, cols_n * SUB
    ex, ey = nx + 2 * RAD, ny + 2 * RAD
    load = pltpu.make_async_copy(map_hbm, map_v, in_sem)
    load.start()

    def atom(ai, bi):
        data = atoms_ref[ai, bi]
        cx = data[0:1] * float(SUB)
        cy = data[1:2] * float(SUB)
        cz = data[2:3] * float(DEPTH)
        sharp = 0.5 / (data[3:4] / EIGHT_PI_SQ + BLUR_VAR)
        return cx, cy, cz, sharp, data[4:5]

    def clear(i, _):
        field[i] = jnp.zeros((ey, DEPTH), jnp.float32)
        return 0

    lax.fori_loop(0, ex, clear, 0)

    def render(ai, bi, p0, p_n, j0, j_n):
        cx, cy, cz, sharp, weight = atom(ai, bi)
        vx = value_only(cx, sharp, p_n, p0 - RAD) * weight
        vy = value_only(cy, sharp, 8 * j_n, 8 * j0 - RAD)
        z_hi, z_lo = split(value_only(cz, sharp, DEPTH, 0))
        weights = jnp.concatenate(
            [jnp.concatenate([z_hi, z_hi], 1), jnp.concatenate([z_lo, z_lo], 1)], 0
        )
        rows = []
        for p in range(p_n):
            for j in range(j_n):
                rows.append(vx[p : p + 1] * vy[8 * j : 8 * j + 8])
        plane_hi, plane_lo = split(jnp.concatenate(rows, 0))
        plane = jnp.concatenate([plane_hi, plane_lo], 1)
        both = lax.dot_general(
            plane, weights, (((1,), (1,)), ((), ())), preferred_element_type=jnp.float32
        )
        total = both[:, :DEPTH] + both[:, DEPTH:]
        x0 = SUB * (ai - 1) + p0
        y0 = SUB * (bi - 1) + 8 * j0
        if not isinstance(y0, int):
            y0 = pl.multiple_of(y0, 8)
        for p in range(p_n):
            field[x0 + p, pl.ds(y0, 8 * j_n), :] += total[8 * j_n * p : 8 * j_n * (p + 1)]

    def own(i, _):
        render(i // cols_n + 1, i % cols_n + 1, 0, TILE, 0, 3)
        return 0

    lax.fori_loop(0, rows_n * cols_n, own, 0)

    def x_side(i, _):
        render(0, i + 1, SUB, 8, 0, 3)
        render(rows_n + 1, i + 1, 0, 8, 0, 3)
        return 0

    lax.fori_loop(0, cols_n, x_side, 0)

    def y_side(i, _):
        render(i + 1, 0, 0, TILE, 2, 1)
        render(i + 1, cols_n + 1, 0, TILE, 0, 1)
        return 0

    lax.fori_loop(0, rows_n, y_side, 0)
    for ai, p0 in ((0, SUB), (rows_n + 1, 0)):
        for bi, j0 in ((0, 2), (cols_n + 1, 0)):
            render(ai, bi, p0, 8, j0, 1)

    load.wait()

    def brick(i, _):
        inside = field[i + RAD, RAD : RAD + ny, :] - map_v[i].astype(jnp.float32)
        field[i + RAD, RAD : RAD + ny, :] = inside
        out_v[i] = inside.astype(jnp.bfloat16)
        return 0

    lax.fori_loop(0, nx, brick, 0)
    store = pltpu.make_async_copy(out_v, out_hbm, out_sem)
    store.start()

    def y_rim(i, _):
        rim = yrim_ref[i]
        field[i, 0:RAD, :] = valid_ref[2] * (field[i, 0:RAD, :] - rim[0:RAD])
        field[i, RAD + ny : ey, :] = valid_ref[3] * (field[i, RAD + ny : ey, :] - rim[RAD : 2 * RAD])
        return 0

    lax.fori_loop(0, ex, y_rim, 0)
    for i in range(RAD):
        for side, row in ((0, i), (1, RAD + nx + i)):
            field[row, RAD : RAD + ny, :] -= xrim_ref[side, i]
            field[row] = valid_ref[side] * field[row]

    def pack(i, _):
        for j in range(ey // 8):
            pair = jnp.concatenate(
                [field[2 * i, 8 * j : 8 * j + 8, :], field[2 * i + 1, 8 * j : 8 * j + 8, :]], 0
            )
            hi, lo = split(pair)
            pieces[i, 16 * j : 16 * j + 16, :] = jnp.concatenate([hi, lo], 1)
        return 0

    lax.fori_loop(0, ex // 2, pack, 0)

    def gradient(i, _):
        a, b = i // cols_n, i % cols_n
        cx, cy, cz, sharp, weight = atom(a + 1, b + 1)
        for k, kind in enumerate(all_kinds(cx, sharp, TILE, -RAD)):
            prof_x[k] = kind
        vy, sy, wy = all_kinds(cy, sharp, TILE, -RAD)
        vz, sz, wz = all_kinds(cz, sharp, DEPTH, 0)
        vz_hi, vz_lo = split(vz)
        sz_hi, sz_lo = split(sz)
        wz_hi = wz.astype(jnp.bfloat16)
        tile = pieces[pl.ds(8 * a, TILE // 2), pl.ds(pl.multiple_of(32 * b, 32), 2 * TILE), :]
        tile = tile.reshape(TILE * TILE, 2 * DEPTH)

        def project(rhs):
            return jnp.dot(tile, rhs, preferred_element_type=jnp.float32)

        def twice(top):
            return jnp.concatenate([top, top], 0)

        proj_v = project(twice(jnp.concatenate([vz_hi, vz_lo], 1)))
        proj_s = project(twice(jnp.concatenate([sz_hi, sz_lo], 1)))
        proj_w = project(twice(wz_hi))
        acc = [[jnp.zeros((8, CAP), jnp.float32) for _ in range(3)] for _ in range(4)]
        for p in range(TILE):
            vx = prof_x[0, p : p + 1, :]
            sx = prof_x[1, p : p + 1, :]
            wx = prof_x[2, p : p + 1, :]
            for j in range(3):
                at = ((p // 2) * 3 + j) * 16 + (p % 2) * 8
                base = proj_v[at : at + 8, :CAP] + proj_v[at : at + 8, CAP:]
                lift = proj_s[at : at + 8, :CAP] + proj_s[at : at + 8, CAP:]
                wide = proj_w[at : at + 8]
                acc[0][j] += base * vx
                acc[1][j] += base * sx
                acc[2][j] += lift * vx
                acc[3][j] += base * wx + wide * vx
        g_x = g_y = g_z = g_s = 0.0
        for j in range(3):
            at = slice(8 * j, 8 * j + 8)
            g_x += acc[1][j] * vy[at]
            g_y += acc[0][j] * sy[at]
            g_z += acc[2][j] * vy[at]
            g_s += acc[3][j] * vy[at] + acc[0][j] * wy[at]
        scale = -2.0 * sharp * sharp / EIGHT_PI_SQ
        for k, g in enumerate((g_x, g_y, g_z, g_s)):
            g = weight * jnp.sum(g, axis=0, keepdims=True)
            if k == 3:
                g = g * scale
            grad_ref[k, a, pl.ds(b, 1), :] = g
        return 0

    lax.fori_loop(0, rows_n * cols_n, gradient, 0)
    store.wait()


def local(atom_pos, b_factor, amplitude, counts, density_map):
    rows_n, cols_n = counts.shape
    nx, ny = rows_n * SUB, cols_n * SUB
    ex, ey = nx + 2 * RAD, ny + 2 * RAD
    live = jnp.arange(CAP)[None, None, :] < counts[..., None]
    weight = jnp.where(live, amplitude, 0.0)
    zero = jnp.zeros_like(weight)
    atoms = jnp.stack([atom_pos[0], atom_pos[1], atom_pos[2], b_factor, weight, zero, zero, zero], 2)

    def message(rim, subs):
        return jnp.concatenate([rim.astype(jnp.float32).reshape(-1, DEPTH), subs.reshape(-1, CAP)], 0)

    cut = RAD * ny
    from_low = shift(message(density_map[-RAD:], atoms[-1]), "bx", 1)
    from_high = shift(message(density_map[:RAD], atoms[0]), "bx", -1)
    rim_low, rim_high = from_low[:cut].reshape(RAD, ny, DEPTH), from_high[:cut].reshape(RAD, ny, DEPTH)
    subs_low = from_low[cut:].reshape(1, cols_n, FIELDS, CAP)
    subs_high = from_high[cut:].reshape(1, cols_n, FIELDS, CAP)
    tall = jnp.concatenate([subs_low, atoms, subs_high], 0)

    def edge(array):
        return array.astype(jnp.float32)

    def column(at):
        return jnp.concatenate([rim_low[:, at], edge(density_map[:, at]), rim_high[:, at]], 0)

    cut = RAD * ex
    low = shift(message(column(slice(ny - RAD, ny)), tall[:, -1]), "by", 1)
    high = shift(message(column(slice(0, RAD)), tall[:, 0]), "by", -1)
    left, right = low[:cut].reshape(ex, RAD, DEPTH), high[:cut].reshape(ex, RAD, DEPTH)
    tall_low = low[cut:].reshape(rows_n + 2, 1, FIELDS, CAP)
    tall_high = high[cut:].reshape(rows_n + 2, 1, FIELDS, CAP)
    wide = jnp.concatenate([tall_low, tall, tall_high], 1)
    xrim = jnp.stack([rim_low, rim_high])
    yrim = jnp.concatenate([left, right], 1)
    ix, iy = lax.axis_index("bx"), lax.axis_index("by")
    valid = jnp.stack(
        [ix > 0, ix < lax.axis_size("bx") - 1, iy > 0, iy < lax.axis_size("by") - 1]
    ).astype(jnp.float32)

    vmem = pl.BlockSpec(memory_space=pltpu.VMEM)
    anywhere = pl.BlockSpec(memory_space=pl.ANY)
    residual, gradient = pl.pallas_call(
        functools.partial(kernel, rows_n, cols_n),
        out_shape=(
            jax.ShapeDtypeStruct((nx, ny, DEPTH), jnp.bfloat16),
            jax.ShapeDtypeStruct((4, rows_n, cols_n, CAP), jnp.float32),
        ),
        in_specs=[pl.BlockSpec(memory_space=pltpu.SMEM), vmem, vmem, vmem, anywhere],
        out_specs=(anywhere, vmem),
        scratch_shapes=[
            pltpu.VMEM((ex, ey, DEPTH), jnp.float32),
            pltpu.VMEM((ex // 2, 2 * ey, 2 * DEPTH), jnp.bfloat16),
            pltpu.VMEM((nx, ny, DEPTH), jnp.bfloat16),
            pltpu.VMEM((nx, ny, DEPTH), jnp.bfloat16),
            pltpu.VMEM((3, TILE, CAP), jnp.float32),
            pltpu.SemaphoreType.DMA,
            pltpu.SemaphoreType.DMA,
        ],
        compiler_params=pltpu.CompilerParams(vmem_limit_bytes=48 << 20),
    )(valid, wide, xrim, yrim, density_map)
    return residual, gradient


def solution(mesh):
    return jax.shard_map(
        local,
        mesh=mesh,
        in_specs=(
            P(None, "bx", "by", None),
            P("bx", "by", None),
            P("bx", "by", None),
            P("bx", "by"),
            P("bx", "by", None),
        ),
        out_specs=(P("bx", "by", None), P(None, "bx", "by", None)),
        check_vma=False,
    )
```

```python
import functools
import math

import jax
import jax.numpy as jnp
from jax import lax
from jax.experimental import pallas as pl
from jax.experimental.pallas import tpu as pltpu
from jax.sharding import PartitionSpec as P

SUB = 16
RAD = 4
TILE = 24
CAP = 128
DEPTH = 128
FIELDS = 8

EIGHT_PI_SQ = 8.0 * math.pi**2
BLUR_VAR = 0.5
REACH_SQ = float(RAD * RAD)


def shift(block, axis, step):
    peers = lax.axis_size(axis)
    route = [(i, (i + step) % peers) for i in range(peers)]
    return lax.ppermute(block, axis, route)


def split(value):
    high = value.astype(jnp.bfloat16)
    low = (value - high.astype(jnp.float32)).astype(jnp.bfloat16)
    return high, low


def base_profile(coordinate, sharpness, span, offset):
    grid = (lax.broadcasted_iota(jnp.int32, (span, CAP), 0) + offset).astype(jnp.float32)
    distance = grid - coordinate
    square = distance * distance
    falloff = jnp.maximum(1.0 - square * (1.0 / REACH_SQ), 0.0)
    damped = jnp.exp(-sharpness * square) * falloff
    return distance, square, falloff, damped


def value_only(coordinate, sharpness, span, offset):
    _, _, falloff, damped = base_profile(coordinate, sharpness, span, offset)
    return damped * falloff


def all_kinds(coordinate, sharpness, span, offset):
    distance, square, falloff, damped = base_profile(coordinate, sharpness, span, offset)
    value = damped * falloff
    slope = 2.0 * distance * (sharpness * value + (2.0 / REACH_SQ) * damped)
    width = -square * value
    return value, slope, width


def kernel(
    rows_n, cols_n,
    valid_ref, atoms_ref, xrim_ref, yrim_ref, map_hbm,
    out_hbm, grad_ref,
    field, pieces, map_v, out_v, prof_x, in_sem, out_sem,
):
    nx, ny = rows_n * SUB, cols_n * SUB
    ex, ey = nx + 2 * RAD, ny + 2 * RAD
    load = pltpu.make_async_copy(map_hbm, map_v, in_sem)
    load.start()

    def atom(ai, bi):
        data = atoms_ref[ai, bi]
        cx = data[0:1] * float(SUB)
        cy = data[1:2] * float(SUB)
        cz = data[2:3] * float(DEPTH)
        sharp = 0.5 / (data[3:4] / EIGHT_PI_SQ + BLUR_VAR)
        return cx, cy, cz, sharp, data[4:5]

    def clear(i, _):
        field[i] = jnp.zeros((ey, DEPTH), jnp.float32)
        return 0

    lax.fori_loop(0, ex, clear, 0)

    def render(ai, bi, p0, p_n, j0, j_n):
        cx, cy, cz, sharp, weight = atom(ai, bi)
        vx = value_only(cx, sharp, p_n, p0 - RAD) * weight
        vy = value_only(cy, sharp, 8 * j_n, 8 * j0 - RAD)
        z_hi, z_lo = split(value_only(cz, sharp, DEPTH, 0))
        weights = jnp.concatenate(
            [jnp.concatenate([z_hi, z_hi], 1), jnp.concatenate([z_lo, z_lo], 1)], 0
        )
        rows = []
        for p in range(p_n):
            for j in range(j_n):
                rows.append(vx[p : p + 1] * vy[8 * j : 8 * j + 8])
        plane_hi, plane_lo = split(jnp.concatenate(rows, 0))
        plane = jnp.concatenate([plane_hi, plane_lo], 1)
        both = lax.dot_general(
            plane, weights, (((1,), (1,)), ((), ())), preferred_element_type=jnp.float32
        )
        total = both[:, :DEPTH] + both[:, DEPTH:]
        x0 = SUB * (ai - 1) + p0
        y0 = SUB * (bi - 1) + 8 * j0
        if not isinstance(y0, int):
            y0 = pl.multiple_of(y0, 8)
        for p in range(p_n):
            field[x0 + p, pl.ds(y0, 8 * j_n), :] += total[8 * j_n * p : 8 * j_n * (p + 1)]

    def own(i, _):
        render(i // cols_n + 1, i % cols_n + 1, 0, TILE, 0, 3)
        return 0

    lax.fori_loop(0, rows_n * cols_n, own, 0, unroll=4)

    def x_side(i, _):
        render(0, i + 1, SUB, 8, 0, 3)
        render(rows_n + 1, i + 1, 0, 8, 0, 3)
        return 0

    lax.fori_loop(0, cols_n, x_side, 0, unroll=4)

    def y_side(i, _):
        render(i + 1, 0, 0, TILE, 2, 1)
        render(i + 1, cols_n + 1, 0, TILE, 0, 1)
        return 0

    lax.fori_loop(0, rows_n, y_side, 0, unroll=4)
    for ai, p0 in ((0, SUB), (rows_n + 1, 0)):
        for bi, j0 in ((0, 2), (cols_n + 1, 0)):
            render(ai, bi, p0, 8, j0, 1)

    load.wait()

    def brick(i, _):
        inside = field[i + RAD, RAD : RAD + ny, :] - map_v[i].astype(jnp.float32)
        field[i + RAD, RAD : RAD + ny, :] = inside
        out_v[i] = inside.astype(jnp.bfloat16)
        return 0

    lax.fori_loop(0, nx, brick, 0, unroll=4)
    store = pltpu.make_async_copy(out_v, out_hbm, out_sem)
    store.start()

    def y_rim(i, _):
        rim = yrim_ref[i]
        field[i, 0:RAD, :] = valid_ref[2] * (field[i, 0:RAD, :] - rim[0:RAD])
        field[i, RAD + ny : ey, :] = valid_ref[3] * (field[i, RAD + ny : ey, :] - rim[RAD : 2 * RAD])
        return 0

    lax.fori_loop(0, ex, y_rim, 0)
    for i in range(RAD):
        for side, row in ((0, i), (1, RAD + nx + i)):
            field[row, RAD : RAD + ny, :] -= xrim_ref[side, i]
            field[row] = valid_ref[side] * field[row]

    def pack(i, _):
        for j in range(ey // 8):
            pair = jnp.concatenate(
                [field[2 * i, 8 * j : 8 * j + 8, :], field[2 * i + 1, 8 * j : 8 * j + 8, :]], 0
            )
            hi, lo = split(pair)
            pieces[i, 16 * j : 16 * j + 16, :] = jnp.concatenate([hi, lo], 1)
        return 0

    lax.fori_loop(0, ex // 2, pack, 0, unroll=2)

    def gradient(i, _):
        a, b = i // cols_n, i % cols_n
        cx, cy, cz, sharp, weight = atom(a + 1, b + 1)
        for k, kind in enumerate(all_kinds(cx, sharp, TILE, -RAD)):
            prof_x[k] = kind
        vy, sy, wy = all_kinds(cy, sharp, TILE, -RAD)
        vz, sz, wz = all_kinds(cz, sharp, DEPTH, 0)
        vz_hi, vz_lo = split(vz)
        sz_hi, sz_lo = split(sz)
        wz_hi = wz.astype(jnp.bfloat16)
        tile = pieces[pl.ds(8 * a, TILE // 2), pl.ds(pl.multiple_of(32 * b, 32), 2 * TILE), :]
        tile = tile.reshape(TILE * TILE, 2 * DEPTH)

        def project(rhs):
            return jnp.dot(tile, rhs, preferred_element_type=jnp.float32)

        def twice(top):
            return jnp.concatenate([top, top], 0)

        proj_v = project(twice(jnp.concatenate([vz_hi, vz_lo], 1)))
        proj_s = project(twice(jnp.concatenate([sz_hi, sz_lo], 1)))
        proj_w = project(twice(wz_hi))
        acc = [[jnp.zeros((8, CAP), jnp.float32) for _ in range(3)] for _ in range(4)]
        for p in range(TILE):
            vx = prof_x[0, p : p + 1, :]
            sx = prof_x[1, p : p + 1, :]
            wx = prof_x[2, p : p + 1, :]
            for j in range(3):
                at = ((p // 2) * 3 + j) * 16 + (p % 2) * 8
                base = proj_v[at : at + 8, :CAP] + proj_v[at : at + 8, CAP:]
                lift = proj_s[at : at + 8, :CAP] + proj_s[at : at + 8, CAP:]
                wide = proj_w[at : at + 8]
                acc[0][j] += base * vx
                acc[1][j] += base * sx
                acc[2][j] += lift * vx
                acc[3][j] += base * wx + wide * vx
        g_x = g_y = g_z = g_s = 0.0
        for j in range(3):
            at = slice(8 * j, 8 * j + 8)
            g_x += acc[1][j] * vy[at]
            g_y += acc[0][j] * sy[at]
            g_z += acc[2][j] * vy[at]
            g_s += acc[3][j] * vy[at] + acc[0][j] * wy[at]
        scale = -2.0 * sharp * sharp / EIGHT_PI_SQ
        for k, g in enumerate((g_x, g_y, g_z, g_s)):
            g = weight * jnp.sum(g, axis=0, keepdims=True)
            if k == 3:
                g = g * scale
            grad_ref[k, a, pl.ds(b, 1), :] = g
        return 0

    lax.fori_loop(0, rows_n * cols_n, gradient, 0, unroll=8)
    store.wait()


def local(atom_pos, b_factor, amplitude, counts, density_map):
    rows_n, cols_n = counts.shape
    nx, ny = rows_n * SUB, cols_n * SUB
    ex, ey = nx + 2 * RAD, ny + 2 * RAD
    ix, iy = lax.axis_index("bx"), lax.axis_index("by")
    valid = jnp.stack(
        [ix > 0, ix < lax.axis_size("bx") - 1, iy > 0, iy < lax.axis_size("by") - 1]
    ).astype(jnp.float32)
    live = jnp.arange(CAP)[None, None, :] < counts[..., None]
    weight = jnp.where(live, amplitude, 0.0)
    zero = jnp.zeros_like(weight)
    atoms = jnp.stack([atom_pos[0], atom_pos[1], atom_pos[2], b_factor, weight, zero, zero, zero], 2)

    def message(rim, subs):
        return jnp.concatenate([rim.astype(jnp.float32).reshape(-1, DEPTH), subs.reshape(-1, CAP)], 0)

    cut = RAD * ny
    from_low = shift(message(density_map[-RAD:], atoms[-1]), "bx", 1)
    from_high = shift(message(density_map[:RAD], atoms[0]), "bx", -1)
    rim_low, rim_high = from_low[:cut].reshape(RAD, ny, DEPTH), from_high[:cut].reshape(RAD, ny, DEPTH)
    subs_low = from_low[cut:].reshape(1, cols_n, FIELDS, CAP)
    subs_high = from_high[cut:].reshape(1, cols_n, FIELDS, CAP)
    tall = jnp.concatenate([subs_low * valid[0], atoms, subs_high * valid[1]], 0)

    def edge(array):
        return array.astype(jnp.float32)

    def column(at):
        return jnp.concatenate([rim_low[:, at], edge(density_map[:, at]), rim_high[:, at]], 0)

    cut = RAD * ex
    low = shift(message(column(slice(ny - RAD, ny)), tall[:, -1]), "by", 1)
    high = shift(message(column(slice(0, RAD)), tall[:, 0]), "by", -1)
    left, right = low[:cut].reshape(ex, RAD, DEPTH), high[:cut].reshape(ex, RAD, DEPTH)
    tall_low = low[cut:].reshape(rows_n + 2, 1, FIELDS, CAP)
    tall_high = high[cut:].reshape(rows_n + 2, 1, FIELDS, CAP)
    wide = jnp.concatenate([tall_low * valid[2], tall, tall_high * valid[3]], 1)
    xrim = jnp.stack([rim_low, rim_high])
    yrim = jnp.concatenate([left, right], 1)
    vmem = pl.BlockSpec(memory_space=pltpu.VMEM)
    anywhere = pl.BlockSpec(memory_space=pl.ANY)
    residual, gradient = pl.pallas_call(
        functools.partial(kernel, rows_n, cols_n),
        out_shape=(
            jax.ShapeDtypeStruct((nx, ny, DEPTH), jnp.bfloat16),
            jax.ShapeDtypeStruct((4, rows_n, cols_n, CAP), jnp.float32),
        ),
        in_specs=[pl.BlockSpec(memory_space=pltpu.SMEM), vmem, vmem, vmem, anywhere],
        out_specs=(anywhere, vmem),
        scratch_shapes=[
            pltpu.VMEM((ex, ey, DEPTH), jnp.float32),
            pltpu.VMEM((ex // 2, 2 * ey, 2 * DEPTH), jnp.bfloat16),
            pltpu.VMEM((nx, ny, DEPTH), jnp.bfloat16),
            pltpu.VMEM((nx, ny, DEPTH), jnp.bfloat16),
            pltpu.VMEM((3, TILE, CAP), jnp.float32),
            pltpu.SemaphoreType.DMA,
            pltpu.SemaphoreType.DMA,
        ],
        compiler_params=pltpu.CompilerParams(vmem_limit_bytes=48 << 20),
    )(valid, wide, xrim, yrim, density_map)
    return residual, gradient


def solution(mesh):
    return jax.shard_map(
        local,
        mesh=mesh,
        in_specs=(
            P(None, "bx", "by", None),
            P("bx", "by", None),
            P("bx", "by", None),
            P("bx", "by"),
            P("bx", "by", None),
        ),
        out_specs=(P("bx", "by", None), P(None, "bx", "by", None)),
        check_vma=False,
    )
```

```python
import functools
import math

import jax
import jax.numpy as jnp
from jax import lax
from jax.experimental import pallas as pl
from jax.experimental.pallas import tpu as pltpu
from jax.sharding import PartitionSpec as P

SUB = 16
RAD = 4
TILE = 24
CAP = 128
DEPTH = 128
FIELDS = 5
BAND = 24

EIGHT_PI_SQ = 8.0 * math.pi**2
BLUR_VAR = 0.5
REACH_SQ = float(RAD * RAD)
VMEM_LIMIT = 18 << 20


def shift(block, axis, step):
    peers = lax.axis_size(axis)
    route = [(i, (i + step) % peers) for i in range(peers)]
    return lax.ppermute(block, axis, route)


def swap(block, odd):
    nx, ny = lax.axis_size("bx"), lax.axis_size("by")
    route = []
    for x in range(nx):
        for y in range(ny):
            to_x, to_y = x, (y ^ 1 if not odd else ((y + 1) ^ 1) - 1)
            if not 0 <= to_y < ny:
                to_x, to_y = x ^ 1, y
            route.append((x * ny + y, to_x * ny + to_y))
    return lax.ppermute(block, ("bx", "by"), route)


def neighbours(low, high):
    even = lax.axis_index("by") % 2 == 0
    first = swap(jnp.where(even, high, low), False)
    second = swap(jnp.where(even, low, high), True)
    return jnp.where(even, second, first), jnp.where(even, first, second)


def split(value):
    high = value.astype(jnp.bfloat16)
    low = (value - high.astype(jnp.float32)).astype(jnp.bfloat16)
    return high, low


def base_profile(coordinate, sharpness, span, offset):
    grid = (lax.broadcasted_iota(jnp.int32, (span, CAP), 0) + offset).astype(jnp.float32)
    distance = grid - coordinate
    square = distance * distance
    falloff = jnp.maximum(1.0 - square * (1.0 / REACH_SQ), 0.0)
    damped = jnp.exp(-sharpness * square) * falloff
    return distance, square, falloff, damped


def value_only(coordinate, sharpness, span, offset):
    _, _, falloff, damped = base_profile(coordinate, sharpness, span, offset)
    return damped * falloff


def all_kinds(coordinate, sharpness, span, offset):
    distance, square, falloff, damped = base_profile(coordinate, sharpness, span, offset)
    value = damped * falloff
    slope = 2.0 * distance * (sharpness * value + (2.0 / REACH_SQ) * damped)
    width = -square * value
    return value, slope, width


def terms(x, y, z, b_factor):
    cx, cy, cz = x * float(SUB), y * float(SUB), z * float(DEPTH)
    return cx, cy, cz, 0.5 / (b_factor / EIGHT_PI_SQ + BLUR_VAR)


def fetch(pairs, sems):
    copies = [pltpu.make_async_copy(a, b, sems.at[i]) for i, (a, b) in enumerate(pairs)]
    for copy in copies:
        copy.start()
    return copies


def finish(copies):
    for copy in copies:
        copy.wait()


def masked(amplitude, count):
    slot = lax.broadcasted_iota(jnp.int32, (1, CAP), 1)
    return jnp.where(slot < count, amplitude, 0.0)


def own_atom(counts_ref, pos_ref, bfac_ref, amp_ref, a, b):
    row = pl.ds(b, 1)
    found = terms(*(pos_ref[k, a, row, :] for k in range(3)), bfac_ref[a, row, :])
    return found + (masked(amp_ref[a, row, :], counts_ref[a, b]),)


def sent_atom(message, start, stride, index, valid):
    row = [message[pl.ds(start + k * stride + index, 1), :] for k in range(FIELDS)]
    return terms(*row[:4]) + (row[4] * valid,)


def rendered(atom, p0, p_n, j0, j_n):
    cx, cy, cz, sharp, weight = atom
    vx = value_only(cx, sharp, p_n, p0 - RAD) * weight
    vy = value_only(cy, sharp, 8 * j_n, 8 * j0 - RAD)
    z_hi, z_lo = split(value_only(cz, sharp, DEPTH, 0))
    weights = jnp.concatenate(
        [jnp.concatenate([z_hi, z_hi], 1), jnp.concatenate([z_lo, z_lo], 1)], 0
    )
    rows = []
    for p in range(p_n):
        for j in range(j_n):
            rows.append(vx[p : p + 1] * vy[8 * j : 8 * j + 8])
    plane_hi, plane_lo = split(jnp.concatenate(rows, 0))
    plane = jnp.concatenate([plane_hi, plane_lo], 1)
    both = lax.dot_general(
        plane, weights, (((1,), (1,)), ((), ())), preferred_element_type=jnp.float32
    )
    total = both[:, :DEPTH] + both[:, DEPTH:]
    return [total[8 * j_n * p : 8 * j_n * (p + 1)] for p in range(p_n)]


def packed(first, second):
    hi, lo = split(jnp.concatenate([first, second], 0))
    return jnp.concatenate([hi, lo], 1)


def tile_gradient(atom, pieces, prof_x, grad_ref, a, b):
    cx, cy, cz, sharp, weight = atom
    for k, kind in enumerate(all_kinds(cx, sharp, TILE, -RAD)):
        prof_x[k] = kind
    vy, sy, wy = all_kinds(cy, sharp, TILE, -RAD)
    vz, sz, wz = all_kinds(cz, sharp, DEPTH, 0)
    vz_hi, vz_lo = split(vz)
    sz_hi, sz_lo = split(sz)
    wz_hi = wz.astype(jnp.bfloat16)
    tile = pieces[pl.ds(8 * a, TILE // 2), pl.ds(pl.multiple_of(32 * b, 32), 2 * TILE), :]
    tile = tile.reshape(TILE * TILE, 2 * DEPTH)

    def project(rhs):
        return jnp.dot(tile, jnp.concatenate([rhs, rhs], 0), preferred_element_type=jnp.float32)

    proj_v = project(jnp.concatenate([vz_hi, vz_lo], 1))
    proj_s = project(jnp.concatenate([sz_hi, sz_lo], 1))
    proj_w = project(wz_hi)
    acc = [[jnp.zeros((8, CAP), jnp.float32) for _ in range(3)] for _ in range(4)]
    for p in range(TILE):
        vx = prof_x[0, p : p + 1, :]
        sx = prof_x[1, p : p + 1, :]
        wx = prof_x[2, p : p + 1, :]
        for j in range(3):
            at = ((p // 2) * 3 + j) * 16 + (p % 2) * 8
            base = proj_v[at : at + 8, :CAP] + proj_v[at : at + 8, CAP:]
            lift = proj_s[at : at + 8, :CAP] + proj_s[at : at + 8, CAP:]
            wide = proj_w[at : at + 8]
            acc[0][j] += base * vx
            acc[1][j] += base * sx
            acc[2][j] += lift * vx
            acc[3][j] += base * wx + wide * vx
    g_x = g_y = g_z = g_s = 0.0
    for j in range(3):
        at = slice(8 * j, 8 * j + 8)
        g_x += acc[1][j] * vy[at]
        g_y += acc[0][j] * sy[at]
        g_z += acc[2][j] * vy[at]
        g_s += acc[3][j] * vy[at] + acc[0][j] * wy[at]
    scale = -2.0 * sharp * sharp / EIGHT_PI_SQ
    for k, g in enumerate((g_x, g_y, g_z, g_s)):
        g = weight * jnp.sum(g, axis=0, keepdims=True)
        if k == 3:
            g = g * scale
        grad_ref[k, a, pl.ds(b, 1), :] = g


def message_kernel(
    rows_n, cols_n,
    counts_hbm, pos_hbm, bfac_hbm, amp_hbm, map_hbm,
    xlow_ref, xhigh_ref, ylow_ref, yhigh_ref,
    counts_ref, pos_ref, bfac_ref, amp_ref, own_sems,
    xrim, yrim, sems,
):
    nx, ny = rows_n * SUB, cols_n * SUB
    held = (counts_ref, pos_ref, bfac_ref, amp_ref)
    fetched = fetch(zip((counts_hbm, pos_hbm, bfac_hbm, amp_hbm), held), own_sems)
    copies = []
    for k, at in enumerate((0, nx - RAD)):
        copies.append(pltpu.make_async_copy(map_hbm.at[pl.ds(at, RAD)], xrim.at[k], sems.at[k]))
    for k, at in enumerate((0, ny - SUB)):
        copies.append(
            pltpu.make_async_copy(map_hbm.at[:, pl.ds(at, SUB)], yrim.at[k], sems.at[2 + k])
        )
    for copy in copies:
        copy.start()

    def atoms(out, start, stride, index, a, b):
        fields = [pos_ref[k, a, b : b + 1, :] for k in range(3)] + [bfac_ref[a, b : b + 1, :]]
        fields.append(masked(amp_ref[a, b : b + 1, :], counts_ref[a, b]))
        for k, value in enumerate(fields):
            out[start + k * stride + index : start + k * stride + index + 1, :] = value

    finish(fetched)
    for b in range(cols_n):
        atoms(xlow_ref, RAD * ny, cols_n, b, 0, b)
        atoms(xhigh_ref, RAD * ny, cols_n, b, rows_n - 1, b)
    for out in (ylow_ref, yhigh_ref):
        out[nx * RAD :, :] = jnp.zeros((BAND, CAP), jnp.float32)
    for a in range(rows_n):
        atoms(ylow_ref, RAD * nx, rows_n, a, a, 0)
        atoms(yhigh_ref, RAD * nx, rows_n, a, a, cols_n - 1)
    for copy in copies:
        copy.wait()
    for k, out in enumerate((xlow_ref, xhigh_ref)):
        for i in range(RAD):
            out[ny * i : ny * (i + 1), :] = xrim[k, i].astype(jnp.float32)
    for i in range(nx):
        ylow_ref[RAD * i : RAD * (i + 1), :] = yrim[0, i].astype(jnp.float32)[:RAD]
        yhigh_ref[RAD * i : RAD * (i + 1), :] = yrim[1, i].astype(jnp.float32)[SUB - RAD :]


def inner_kernel(
    rows_n, cols_n,
    counts_hbm, pos_hbm, bfac_hbm, amp_hbm, map_hbm,
    out_hbm, pieces_hbm, xband_hbm, yband_hbm, grad_ref,
    counts_ref, pos_ref, bfac_ref, amp_ref, own_sems,
    field, pieces, map_v, out_v, prof_x, in_sem, out_sems,
):
    nx, ny = rows_n * SUB, cols_n * SUB
    ex, ey = nx + 2 * RAD, ny + 2 * RAD
    held = (counts_ref, pos_ref, bfac_ref, amp_ref)
    fetched = fetch(zip((counts_hbm, pos_hbm, bfac_hbm, amp_hbm), held), own_sems)
    load = pltpu.make_async_copy(map_hbm, map_v, in_sem)
    load.start()

    def clear(i, _):
        field[i] = jnp.zeros((ey, DEPTH), jnp.float32)
        return 0

    lax.fori_loop(0, ex, clear, 0)
    finish(fetched)
    atom_at = functools.partial(own_atom, counts_ref, pos_ref, bfac_ref, amp_ref)

    def own(i, _):
        a, b = i // cols_n, i % cols_n
        y0 = pl.multiple_of(SUB * b, SUB)
        for p, row in enumerate(rendered(atom_at(a, b), 0, TILE, 0, 3)):
            field[SUB * a + p, pl.ds(y0, TILE), :] += row
        return 0

    lax.fori_loop(0, rows_n * cols_n, own, 0, unroll=4)
    load.wait()

    def brick(i, _):
        inside = field[i + RAD, RAD : RAD + ny, :] - map_v[i].astype(jnp.float32)
        field[i + RAD, RAD : RAD + ny, :] = inside
        out_v[i] = inside.astype(jnp.bfloat16)
        return 0

    lax.fori_loop(0, nx, brick, 0, unroll=4)
    rest = pl.ds(2 * RAD, nx - 2 * RAD)
    pairs = [(out_v, out_hbm)]
    for k in range(2):
        pairs.append((field.at[pl.ds((ex - 2 * RAD) * k, 2 * RAD)], xband_hbm.at[k]))
        pairs.append((field.at[rest, pl.ds((ey - BAND) * k, BAND)], yband_hbm.at[k]))
    stores = fetch(pairs, out_sems)

    def pack(i, _):
        for j in range(ey // 8):
            rows = pl.ds(8 * j, 8)
            pieces[i, 16 * j : 16 * j + 16, :] = packed(field[2 * i, rows, :], field[2 * i + 1, rows, :])
        return 0

    lax.fori_loop(RAD, ex // 2 - RAD, pack, 0, unroll=2)
    kept = (pl.ds(RAD, ex // 2 - 2 * RAD), pl.ds(SUB, 2 * ey - 2 * SUB))
    last = pltpu.make_async_copy(pieces.at[kept], pieces_hbm, in_sem)
    last.start()

    def gradient(i, _):
        a, b = i // (cols_n - 2) + 1, i % (cols_n - 2) + 1
        tile_gradient(atom_at(a, b), pieces, prof_x, grad_ref, a, b)
        return 0

    lax.fori_loop(0, (rows_n - 2) * (cols_n - 2), gradient, 0, unroll=6)
    finish(stores)
    last.wait()


def sides_kernel(
    rows_n, cols_n,
    valid_ref, xlow_ref, xhigh_ref, ylow_ref, yhigh_ref, xband_hbm, yband_hbm,
    xband, yband,
    xfield, yfield, sems,
):
    nx, ny = rows_n * SUB, cols_n * SUB
    ex, ey = nx + 2 * RAD, ny + 2 * RAD
    fetched = fetch(((xband_hbm, xfield), (yband_hbm, yfield)), sems)
    xband[...] = jnp.zeros_like(xband)
    yband[...] = jnp.zeros_like(yband)

    def x_side(b, _):
        y0 = pl.multiple_of(SUB * b, SUB)
        for k, (message, p0) in enumerate(((xlow_ref, SUB), (xhigh_ref, 0))):
            atom = sent_atom(message, RAD * ny, cols_n, b, valid_ref[k])
            for p, row in enumerate(rendered(atom, p0, 2 * RAD, 0, 3)):
                xband[k, p, pl.ds(y0, TILE), :] += row
        return 0

    lax.fori_loop(0, cols_n, x_side, 0, unroll=4)
    for a in range(rows_n):
        for k, (message, j0, y0) in enumerate(((ylow_ref, 2, 0), (yhigh_ref, 0, ey - 8))):
            atom = sent_atom(message, RAD * nx, rows_n, a, valid_ref[2 + k])
            for p, row in enumerate(rendered(atom, 0, TILE, j0, 1)):
                x = SUB * a + p
                if x < 2 * RAD:
                    xband[0, x, y0 : y0 + 8, :] += row
                elif x >= ex - 2 * RAD:
                    xband[1, x - (ex - 2 * RAD), y0 : y0 + 8, :] += row
                else:
                    yband[k, x - 2 * RAD, (BAND - 8) * k : (BAND - 8) * k + 8, :] += row
    finish(fetched)
    xband[...] += xfield[...]
    yband[...] += yfield[...]


def outer_kernel(
    rows_n, cols_n,
    valid_ref, counts_hbm, pos_hbm, bfac_hbm, amp_hbm,
    xlow_ref, xhigh_ref, ylow_ref, yhigh_ref, clow_ref, chigh_ref,
    xband_in, yband_in, pieces_hbm, grad_in, out_in,
    out_hbm, grad_ref,
    counts_ref, pos_ref, bfac_ref, amp_ref, own_sems,
    xband, yband, pieces, xout, yout, prof_x, sems,
):
    nx, ny = rows_n * SUB, cols_n * SUB
    ex, ey = nx + 2 * RAD, ny + 2 * RAD
    kept = (pl.ds(RAD, ex // 2 - 2 * RAD), pl.ds(SUB, 2 * ey - 2 * SUB))
    held = (counts_ref, pos_ref, bfac_ref, amp_ref, pieces.at[kept])
    sources = (counts_hbm, pos_hbm, bfac_hbm, amp_hbm, pieces_hbm)
    fetched = fetch(zip(sources, held), own_sems)
    xband[...] = xband_in[...]
    yband[...] = yband_in[...]
    grad_ref[...] = grad_in[...]
    corner = RAD * RAD + FIELDS
    for ky, (message, j0, y0) in enumerate(((clow_ref, 2, 0), (chigh_ref, 0, ey - 8))):
        for kx, p0 in enumerate((SUB, 0)):
            ok = valid_ref[kx] * valid_ref[2 + ky]
            atom = sent_atom(message, corner * kx + RAD * RAD, 1, 0, ok)
            for p, row in enumerate(rendered(atom, p0, 2 * RAD, j0, 1)):
                xband[kx, p, y0 : y0 + 8, :] += row
    for kx, message in enumerate((xlow_ref, xhigh_ref)):
        for i in range(RAD):
            row = RAD * kx + i
            xband[kx, row, RAD : RAD + ny, :] -= message[ny * i : ny * (i + 1), :]
            for ky, sent in enumerate((clow_ref, chigh_ref)):
                y0 = (ey - RAD) * ky
                at = corner * kx + RAD * i
                xband[kx, row, y0 : y0 + RAD, :] -= sent[at : at + RAD, :]
            xband[kx, row] = valid_ref[kx] * xband[kx, row]
    for ky, message in enumerate((ylow_ref, yhigh_ref)):
        y0 = (ey - RAD) * ky
        for kx in range(2):
            for i in range(RAD):
                row = RAD * (1 - kx) + i
                at = RAD * ((nx - RAD) * kx + i)
                xband[kx, row, y0 : y0 + RAD, :] -= message[at : at + RAD, :]
            for i in range(2 * RAD):
                xband[kx, i, y0 : y0 + RAD, :] = valid_ref[2 + ky] * xband[kx, i, y0 : y0 + RAD, :]
        y0 = (BAND - RAD) * ky
        for i in range(nx - 2 * RAD):
            at = RAD * (RAD + i)
            inside = yband[ky, i, y0 : y0 + RAD, :] - message[at : at + RAD, :]
            yband[ky, i, y0 : y0 + RAD, :] = valid_ref[2 + ky] * inside

    stores = []
    for kx in range(2):
        for i in range(RAD):
            xout[kx, i] = xband[kx, RAD * (1 - kx) + i, RAD : RAD + ny, :].astype(jnp.bfloat16)
        stores.append(
            pltpu.make_async_copy(
                xout.at[kx], out_hbm.at[pl.ds((nx - RAD) * kx, RAD)], sems.at[kx]
            )
        )
    for ky in range(2):
        for i in range(nx - 2 * RAD):
            yout[ky, i] = yband[ky, i, RAD : RAD + SUB, :].astype(jnp.bfloat16)
        stores.append(
            pltpu.make_async_copy(
                yout.at[ky],
                out_hbm.at[pl.ds(RAD, nx - 2 * RAD), pl.ds((ny - SUB) * ky, SUB)],
                sems.at[2 + ky],
            )
        )
    for store in stores:
        store.start()
    for kx in range(2):
        for i in range(RAD):
            for j in range(ey // 8):
                rows = slice(8 * j, 8 * j + 8)
                pieces[(ex // 2 - RAD) * kx + i, 16 * j : 16 * j + 16, :] = packed(
                    xband[kx, 2 * i, rows, :], xband[kx, 2 * i + 1, rows, :]
                )
    for ky in range(2):
        rows = slice((BAND - 8) * ky, (BAND - 8) * ky + 8)
        at = 2 * (ey - 8) * ky
        for i in range(nx // 2 - RAD):
            pieces[RAD + i, at : at + 16, :] = packed(
                yband[ky, 2 * i, rows, :], yband[ky, 2 * i + 1, rows, :]
            )
    atom_at = functools.partial(own_atom, counts_ref, pos_ref, bfac_ref, amp_ref)
    finish(fetched)

    def x_edges(i, _):
        a, b = (i // cols_n) * (rows_n - 1), i % cols_n
        tile_gradient(atom_at(a, b), pieces, prof_x, grad_ref, a, b)
        return 0

    def y_edges(i, _):
        a, b = i // 2 + 1, (i % 2) * (cols_n - 1)
        tile_gradient(atom_at(a, b), pieces, prof_x, grad_ref, a, b)
        return 0

    lax.fori_loop(0, 2 * cols_n, x_edges, 0, unroll=8)
    lax.fori_loop(0, 2 * (rows_n - 2), y_edges, 0, unroll=4)
    for store in stores:
        store.wait()


def call(body, sizes, outs, in_specs, out_specs, scratch, cost, aliases=None):
    return pl.pallas_call(
        functools.partial(body, *sizes),
        out_shape=outs,
        in_specs=in_specs,
        out_specs=out_specs,
        scratch_shapes=scratch,
        input_output_aliases=aliases or {},
        cost_estimate=pl.CostEstimate(flops=cost, bytes_accessed=1 << 20, transcendentals=0),
        compiler_params=pltpu.CompilerParams(vmem_limit_bytes=VMEM_LIMIT),
    )


def local(atom_pos, b_factor, amplitude, counts, density_map):
    sizes = rows_n, cols_n = counts.shape
    nx, ny = rows_n * SUB, cols_n * SUB
    ex, ey = nx + 2 * RAD, ny + 2 * RAD
    ix, iy = lax.axis_index("bx"), lax.axis_index("by")
    valid = jnp.stack(
        [ix > 0, ix < lax.axis_size("bx") - 1, iy > 0, iy < lax.axis_size("by") - 1]
    ).astype(jnp.float32)
    f32, bf16 = jnp.float32, jnp.bfloat16
    shape = jax.ShapeDtypeStruct
    vmem = pl.BlockSpec(memory_space=pltpu.VMEM)
    smem = pl.BlockSpec(memory_space=pltpu.SMEM)
    hbm = pl.BlockSpec(memory_space=pltpu.HBM)
    own_scratch = [
        pltpu.SMEM(counts.shape, jnp.int32),
        pltpu.VMEM(atom_pos.shape, f32),
        pltpu.VMEM(b_factor.shape, f32),
        pltpu.VMEM(amplitude.shape, f32),
        pltpu.SemaphoreType.DMA((5,)),
    ]
    own = tuple(
        pltpu.with_memory_space_constraint(array, pltpu.HBM)
        for array in (counts, atom_pos, b_factor, amplitude)
    )
    density_map = pltpu.with_memory_space_constraint(density_map, pltpu.HBM)

    xsize, ysize = RAD * ny + FIELDS * cols_n, RAD * nx + BAND
    xlow, xhigh, ylow, yhigh = call(
        message_kernel,
        sizes,
        (shape((xsize, CAP), f32),) * 2 + (shape((ysize, CAP), f32),) * 2,
        [hbm] * 5,
        (vmem,) * 4,
        own_scratch
        + [
            pltpu.VMEM((2, RAD, ny, DEPTH), bf16),
            pltpu.VMEM((2, nx, SUB, DEPTH), bf16),
            pltpu.SemaphoreType.DMA((4,)),
        ],
        10**6,
    )(*own, density_map)
    from_ylow, from_yhigh = neighbours(ylow, yhigh)
    from_xlow, from_xhigh = shift(xhigh, "bx", 1), shift(xlow, "bx", -1)

    bands = shape((2, 2 * RAD, ey, DEPTH), f32), shape((2, nx - 2 * RAD, BAND, DEPTH), f32)
    residual, *kept, gradient = call(
        inner_kernel,
        sizes,
        (
            shape((nx, ny, DEPTH), bf16),
            pltpu.HBM((ex // 2 - 2 * RAD, 2 * ey - 2 * SUB, 2 * DEPTH), bf16),
            *(pltpu.HBM(band.shape, f32) for band in bands),
            shape((4, rows_n, cols_n, CAP), f32),
        ),
        [hbm] * 5,
        (hbm, hbm, hbm, hbm, vmem),
        own_scratch
        + [
            pltpu.VMEM((ex, ey, DEPTH), f32),
            pltpu.VMEM((ex // 2, 2 * ey, 2 * DEPTH), bf16),
            pltpu.VMEM((nx, ny, DEPTH), bf16),
            pltpu.VMEM((nx, ny, DEPTH), bf16),
            pltpu.VMEM((3, TILE, CAP), f32),
            pltpu.SemaphoreType.DMA,
            pltpu.SemaphoreType.DMA((5,)),
        ],
        10**10,
    )(*own, density_map)

    pieces, xband, yband = (
        pltpu.with_memory_space_constraint(array, pltpu.HBM) for array in kept
    )

    def corners(at, sub):
        parts = []
        for message in (from_xlow, from_xhigh):
            rim = message[: RAD * ny].reshape(RAD, ny, DEPTH)[:, at : at + RAD]
            subs = message[RAD * ny :].reshape(FIELDS, cols_n, CAP)[:, sub]
            parts += [rim.reshape(RAD * RAD, DEPTH), subs]
        return jnp.concatenate(parts, 0)

    from_clow, from_chigh = neighbours(corners(0, 0), corners(ny - RAD, cols_n - 1))

    messages = (from_xlow, from_xhigh, from_ylow, from_yhigh)
    xband, yband = call(
        sides_kernel,
        sizes,
        bands,
        [smem] + [vmem] * 4 + [hbm] * 2,
        (vmem, vmem),
        [pltpu.VMEM(band.shape, f32) for band in bands] + [pltpu.SemaphoreType.DMA((2,))],
        2 * 10**9,
    )(valid, *messages, xband, yband)

    residual, gradient = call(
        outer_kernel,
        sizes,
        (
            shape((nx, ny, DEPTH), bf16),
            shape((4, rows_n, cols_n, CAP), f32),
        ),
        [smem] + [hbm] * 4 + [vmem] * 8 + [hbm, vmem, hbm],
        (hbm, vmem),
        own_scratch
        + [
            pltpu.VMEM(xband.shape, f32),
            pltpu.VMEM(yband.shape, f32),
            pltpu.VMEM((ex // 2, 2 * ey, 2 * DEPTH), bf16),
            pltpu.VMEM((2, RAD, ny, DEPTH), bf16),
            pltpu.VMEM((2, nx - 2 * RAD, SUB, DEPTH), bf16),
            pltpu.VMEM((3, TILE, CAP), f32),
            pltpu.SemaphoreType.DMA((4,)),
        ],
        10**10,
        {15: 0},
    )(valid, *own, *messages, from_clow, from_chigh, xband, yband, pieces, gradient, residual)
    return residual, gradient


def solution(mesh):
    return jax.shard_map(
        local,
        mesh=mesh,
        in_specs=(
            P(None, "bx", "by", None),
            P("bx", "by", None),
            P("bx", "by", None),
            P("bx", "by"),
            P("bx", "by", None),
        ),
        out_specs=(P("bx", "by", None), P(None, "bx", "by", None)),
        check_vma=False,
    )
```

```python
import functools
import math

import jax
import jax.numpy as jnp
from jax import lax
from jax.experimental import pallas as pl
from jax.experimental.pallas import tpu as pltpu
from jax.sharding import PartitionSpec as P

SUB = 16
RAD = 4
TILE = 24
CAP = 128
DEPTH = 128
FIELDS = 5
BAND = 24

EIGHT_PI_SQ = 8.0 * math.pi**2
BLUR_VAR = 0.5
REACH_SQ = float(RAD * RAD)
VMEM_LIMIT = 18 << 20


def shift(block, axis, step):
    peers = lax.axis_size(axis)
    route = [(i, (i + step) % peers) for i in range(peers)]
    return lax.ppermute(block, axis, route)


def swap(block, odd):
    nx, ny = lax.axis_size("bx"), lax.axis_size("by")
    route = []
    for x in range(nx):
        for y in range(ny):
            to_x, to_y = x, (y ^ 1 if not odd else ((y + 1) ^ 1) - 1)
            if not 0 <= to_y < ny:
                to_x, to_y = x ^ 1, y
            route.append((x * ny + y, to_x * ny + to_y))
    return lax.ppermute(block, ("bx", "by"), route)


def is_even():
    return lax.axis_index("by") % 2 == 0


def valid_sides():
    found = []
    for axis in ("bx", "by"):
        at = lax.axis_index(axis)
        found += [at > 0, at < lax.axis_size(axis) - 1]
    return [jnp.where(side, 1.0, 0.0) for side in found]


class Picked:
    def __init__(self, flag, when_true, when_false, start=0):
        self.flag, self.refs, self.start = flag, (when_true, when_false), start

    def rows(self, at, count):
        where = pl.ds(self.start + at, count)
        return jnp.where(self.flag, self.refs[0][where, :], self.refs[1][where, :])


class Plain:
    def __init__(self, ref):
        self.ref = ref

    def rows(self, at, count):
        return self.ref[pl.ds(at, count), :]


def split(value):
    high = value.astype(jnp.bfloat16)
    low = (value - high.astype(jnp.float32)).astype(jnp.bfloat16)
    return high, low


def base_profile(coordinate, sharpness, span, offset):
    grid = (lax.broadcasted_iota(jnp.int32, (span, CAP), 0) + offset).astype(jnp.float32)
    distance = grid - coordinate
    square = distance * distance
    falloff = jnp.maximum(1.0 - square * (1.0 / REACH_SQ), 0.0)
    damped = jnp.exp(-sharpness * square) * falloff
    return distance, square, falloff, damped


def value_only(coordinate, sharpness, span, offset):
    _, _, falloff, damped = base_profile(coordinate, sharpness, span, offset)
    return damped * falloff


def all_kinds(coordinate, sharpness, span, offset):
    distance, square, falloff, damped = base_profile(coordinate, sharpness, span, offset)
    value = damped * falloff
    slope = 2.0 * distance * (sharpness * value + (2.0 / REACH_SQ) * damped)
    width = -square * value
    return value, slope, width


def terms(x, y, z, b_factor):
    cx, cy, cz = x * float(SUB), y * float(SUB), z * float(DEPTH)
    return cx, cy, cz, 0.5 / (b_factor / EIGHT_PI_SQ + BLUR_VAR)


def fetch(pairs, sems):
    copies = [pltpu.make_async_copy(a, b, sems.at[i]) for i, (a, b) in enumerate(pairs)]
    for copy in copies:
        copy.start()
    return copies


def finish(copies):
    for copy in copies:
        copy.wait()


def masked(amplitude, count):
    slot = lax.broadcasted_iota(jnp.int32, (1, CAP), 1)
    return jnp.where(slot < count, amplitude, 0.0)


def own_atom(terms_ref, index):
    return tuple(terms_ref[index, k : k + 1, :] for k in range(FIELDS))


def sent_atom(message, start, stride, index, valid):
    row = [message.rows(start + k * stride + index, 1) for k in range(FIELDS)]
    return terms(*row[:4]) + (row[4] * valid,)


def rendered(atom, p0, p_n, j0, j_n):
    cx, cy, cz, sharp, weight = atom
    vx = value_only(cx, sharp, p_n, p0 - RAD) * weight
    vy = value_only(cy, sharp, 8 * j_n, 8 * j0 - RAD)
    z_hi, z_lo = split(value_only(cz, sharp, DEPTH, 0))
    weights = jnp.concatenate(
        [jnp.concatenate([z_hi, z_hi], 1), jnp.concatenate([z_lo, z_lo], 1)], 0
    )
    rows = []
    for p in range(p_n):
        for j in range(j_n):
            rows.append(vx[p : p + 1] * vy[8 * j : 8 * j + 8])
    plane_hi, plane_lo = split(jnp.concatenate(rows, 0))
    plane = jnp.concatenate([plane_hi, plane_lo], 1)
    both = lax.dot_general(
        plane, weights, (((1,), (1,)), ((), ())), preferred_element_type=jnp.float32
    )
    total = both[:, :DEPTH] + both[:, DEPTH:]
    return [total[8 * j_n * p : 8 * j_n * (p + 1)] for p in range(p_n)]


def packed(first, second):
    hi, lo = split(jnp.concatenate([first, second], 0))
    return jnp.concatenate([hi, lo], 1)


def tile_gradient(atom, pieces, prof_x, grad_ref, a, b):
    cx, cy, cz, sharp, weight = atom
    for k, kind in enumerate(all_kinds(cx, sharp, TILE, -RAD)):
        prof_x[k] = kind
    vy, sy, wy = all_kinds(cy, sharp, TILE, -RAD)
    vz, sz, wz = all_kinds(cz, sharp, DEPTH, 0)
    vz_hi, vz_lo = split(vz)
    sz_hi, sz_lo = split(sz)
    wz_hi = wz.astype(jnp.bfloat16)
    tile = pieces[pl.ds(8 * a, TILE // 2), pl.ds(pl.multiple_of(32 * b, 32), 2 * TILE), :]
    tile = tile.reshape(TILE * TILE, 2 * DEPTH)

    def project(rhs):
        return jnp.dot(tile, jnp.concatenate([rhs, rhs], 0), preferred_element_type=jnp.float32)

    proj_v = project(jnp.concatenate([vz_hi, vz_lo], 1))
    proj_s = project(jnp.concatenate([sz_hi, sz_lo], 1))
    proj_w = project(wz_hi)
    acc = [[jnp.zeros((8, CAP), jnp.float32) for _ in range(3)] for _ in range(4)]
    for p in range(TILE):
        vx = prof_x[0, p : p + 1, :]
        sx = prof_x[1, p : p + 1, :]
        wx = prof_x[2, p : p + 1, :]
        for j in range(3):
            at = ((p // 2) * 3 + j) * 16 + (p % 2) * 8
            base = proj_v[at : at + 8, :CAP] + proj_v[at : at + 8, CAP:]
            lift = proj_s[at : at + 8, :CAP] + proj_s[at : at + 8, CAP:]
            wide = proj_w[at : at + 8]
            acc[0][j] += base * vx
            acc[1][j] += base * sx
            acc[2][j] += lift * vx
            acc[3][j] += base * wx + wide * vx
    g_x = g_y = g_z = g_s = 0.0
    for j in range(3):
        at = slice(8 * j, 8 * j + 8)
        g_x += acc[1][j] * vy[at]
        g_y += acc[0][j] * sy[at]
        g_z += acc[2][j] * vy[at]
        g_s += acc[3][j] * vy[at] + acc[0][j] * wy[at]
    scale = -2.0 * sharp * sharp / EIGHT_PI_SQ
    for k, g in enumerate((g_x, g_y, g_z, g_s)):
        g = weight * jnp.sum(g, axis=0, keepdims=True)
        if k == 3:
            g = g * scale
        grad_ref[k, a, pl.ds(b, 1), :] = g


def message_kernel(
    rows_n, cols_n,
    counts_hbm, pos_hbm, bfac_hbm, amp_hbm, map_hbm,
    xlow_ref, xhigh_ref, first_ref, second_ref, terms_ref,
    counts_ref, pos_ref, bfac_ref, amp_ref, own_sems,
    xrim, yrim, sems,
):
    nx, ny = rows_n * SUB, cols_n * SUB
    held = (counts_ref, pos_ref, bfac_ref, amp_ref)
    fetched = fetch(zip((counts_hbm, pos_hbm, bfac_hbm, amp_hbm), held), own_sems)
    copies = []
    for k, at in enumerate((0, nx - RAD)):
        copies.append(pltpu.make_async_copy(map_hbm.at[pl.ds(at, RAD)], xrim.at[k], sems.at[k]))
    for k, at in enumerate((0, ny - SUB)):
        copies.append(
            pltpu.make_async_copy(map_hbm.at[:, pl.ds(at, SUB)], yrim.at[k], sems.at[2 + k])
        )
    for copy in copies:
        copy.start()

    def fields(a, b):
        found = [pos_ref[k, a, b : b + 1, :] for k in range(3)] + [bfac_ref[a, b : b + 1, :]]
        return found + [masked(amp_ref[a, b : b + 1, :], counts_ref[a, b])]

    def atoms(out, start, stride, index, a, b):
        for k, value in enumerate(fields(a, b)):
            out[start + k * stride + index : start + k * stride + index + 1, :] = value

    finish(fetched)
    for a in range(rows_n):
        found = terms(pos_ref[0, a], pos_ref[1, a], pos_ref[2, a], bfac_ref[a])
        for b in range(cols_n):
            row = slice(b, b + 1)
            weight = masked(amp_ref[a, row, :], counts_ref[a, b])
            terms_ref[a * cols_n + b, 0:FIELDS, :] = jnp.concatenate(
                [value[row] for value in found] + [weight], 0
            )
    for b in range(cols_n):
        atoms(xlow_ref, RAD * ny, cols_n, b, 0, b)
        atoms(xhigh_ref, RAD * ny, cols_n, b, rows_n - 1, b)
    even = is_even()

    def put(where, low, high):
        first_ref[where, :] = jnp.where(even, high, low)
        second_ref[where, :] = jnp.where(even, low, high)

    for out in (first_ref, second_ref):
        out[nx * RAD :, :] = jnp.zeros((BAND, CAP), jnp.float32)
    for a in range(rows_n):
        low, high = fields(a, 0), fields(a, cols_n - 1)
        for k in range(FIELDS):
            at = RAD * nx + k * rows_n + a
            put(slice(at, at + 1), low[k], high[k])
    for copy in copies:
        copy.wait()
    for k, out in enumerate((xlow_ref, xhigh_ref)):
        for i in range(RAD):
            out[ny * i : ny * (i + 1), :] = xrim[k, i].astype(jnp.float32)
    for i in range(nx):
        put(
            slice(RAD * i, RAD * (i + 1)),
            yrim[0, i].astype(jnp.float32)[:RAD],
            yrim[1, i].astype(jnp.float32)[SUB - RAD :],
        )


def inner_kernel(
    rows_n, cols_n,
    terms_ref, map_hbm,
    out_hbm, pieces, xband, yband, grad_ref,
    field, map_v, out_v, prof_x, in_sem, out_sems,
):
    nx, ny = rows_n * SUB, cols_n * SUB
    ex, ey = nx + 2 * RAD, ny + 2 * RAD
    load = pltpu.make_async_copy(map_hbm, map_v, in_sem)
    load.start()

    def clear(i, _):
        field[i] = jnp.zeros((ey, DEPTH), jnp.float32)
        return 0

    lax.fori_loop(0, ex, clear, 0)

    def own(i, _):
        a, b = i // cols_n, i % cols_n
        y0 = pl.multiple_of(SUB * b, SUB)
        for p, row in enumerate(rendered(own_atom(terms_ref, i), 0, TILE, 0, 3)):
            field[SUB * a + p, pl.ds(y0, TILE), :] += row
        return 0

    lax.fori_loop(0, rows_n * cols_n, own, 0, unroll=4)
    load.wait()

    def brick(i, _):
        inside = field[i + RAD, RAD : RAD + ny, :] - map_v[i].astype(jnp.float32)
        field[i + RAD, RAD : RAD + ny, :] = inside
        out_v[i] = inside.astype(jnp.bfloat16)
        return 0

    lax.fori_loop(0, nx, brick, 0, unroll=4)
    rest = pl.ds(2 * RAD, nx - 2 * RAD)
    pairs = [(out_v, out_hbm)]
    for k in range(2):
        pairs.append((field.at[pl.ds((ex - 2 * RAD) * k, 2 * RAD)], xband.at[k]))
        pairs.append((field.at[rest, pl.ds((ey - BAND) * k, BAND)], yband.at[k]))
    stores = fetch(pairs, out_sems)

    def pack(i, _):
        for j in range(ey // 8):
            rows = pl.ds(8 * j, 8)
            pieces[i, 16 * j : 16 * j + 16, :] = packed(field[2 * i, rows, :], field[2 * i + 1, rows, :])
        return 0

    lax.fori_loop(RAD, ex // 2 - RAD, pack, 0, unroll=2)
    def gradient(i, _):
        a, b = i // (cols_n - 2) + 1, i % (cols_n - 2) + 1
        tile_gradient(own_atom(terms_ref, a * cols_n + b), pieces, prof_x, grad_ref, a, b)
        return 0

    lax.fori_loop(0, (rows_n - 2) * (cols_n - 2), gradient, 0, unroll=6)
    finish(stores)


def corner_kernel(rows_n, cols_n, xlow_ref, xhigh_ref, out_ref):
    ny = cols_n * SUB
    at = 0
    for y0, sub in ((0, 0), (ny - RAD, cols_n - 1)):
        for message in (xlow_ref, xhigh_ref):
            for i in range(RAD):
                out_ref[at : at + RAD, :] = message[ny * i + y0 : ny * i + y0 + RAD, :]
                at += RAD
            for k in range(FIELDS):
                row = RAD * ny + k * cols_n + sub
                out_ref[at : at + 1, :] = message[row : row + 1, :]
                at += 1
    out_ref[at:, :] = jnp.zeros((out_ref.shape[0] - at, CAP), jnp.float32)


def sides_kernel(
    rows_n, cols_n,
    xlow_ref, xhigh_ref, first_ref, second_ref, xband_in, yband_in,
    xband, yband,
):
    nx, ny = rows_n * SUB, cols_n * SUB
    ex, ey = nx + 2 * RAD, ny + 2 * RAD
    even, valid = is_even(), valid_sides()
    ylow, yhigh = Picked(even, second_ref, first_ref), Picked(even, first_ref, second_ref)

    def x_side(b, _):
        y0 = pl.multiple_of(SUB * b, SUB)
        for k, (message, p0) in enumerate(((Plain(xlow_ref), SUB), (Plain(xhigh_ref), 0))):
            atom = sent_atom(message, RAD * ny, cols_n, b, valid[k])
            for p, row in enumerate(rendered(atom, p0, 2 * RAD, 0, 3)):
                xband[k, p, pl.ds(y0, TILE), :] += row
        return 0

    lax.fori_loop(0, cols_n, x_side, 0, unroll=4)
    for a in range(rows_n):
        for k, (message, j0, y0) in enumerate(((ylow, 2, 0), (yhigh, 0, ey - 8))):
            atom = sent_atom(message, RAD * nx, rows_n, a, valid[2 + k])
            for p, row in enumerate(rendered(atom, 0, TILE, j0, 1)):
                x = SUB * a + p
                if x < 2 * RAD:
                    xband[0, x, y0 : y0 + 8, :] += row
                elif x >= ex - 2 * RAD:
                    xband[1, x - (ex - 2 * RAD), y0 : y0 + 8, :] += row
                else:
                    yband[k, x - 2 * RAD, (BAND - 8) * k : (BAND - 8) * k + 8, :] += row


def outer_kernel(
    rows_n, cols_n,
    terms_ref, xlow_ref, xhigh_ref, first_ref, second_ref, cfirst_ref, csecond_ref,
    xband_in, yband_in, pieces_in, grad_in, out_in,
    out_hbm, grad_ref, xband, yband, pieces,
    xout, yout, prof_x, sems,
):
    nx, ny = rows_n * SUB, cols_n * SUB
    ex, ey = nx + 2 * RAD, ny + 2 * RAD
    grad_ref[...] = grad_in[...]
    corner = RAD * RAD + FIELDS
    even, valid = is_even(), valid_sides()
    ylow, yhigh = Picked(even, second_ref, first_ref), Picked(even, first_ref, second_ref)
    clow = Picked(even, csecond_ref, cfirst_ref, 2 * corner)
    chigh = Picked(even, cfirst_ref, csecond_ref)
    for ky, (message, j0, y0) in enumerate(((clow, 2, 0), (chigh, 0, ey - 8))):
        for kx, p0 in enumerate((SUB, 0)):
            ok = valid[kx] * valid[2 + ky]
            atom = sent_atom(message, corner * kx + RAD * RAD, 1, 0, ok)
            for p, row in enumerate(rendered(atom, p0, 2 * RAD, j0, 1)):
                xband[kx, p, y0 : y0 + 8, :] += row
    for kx, message in enumerate((xlow_ref, xhigh_ref)):
        for i in range(RAD):
            row = RAD * kx + i
            xband[kx, row, RAD : RAD + ny, :] -= message[ny * i : ny * (i + 1), :]
            for ky, sent in enumerate((clow, chigh)):
                y0 = (ey - RAD) * ky
                at = corner * kx + RAD * i
                xband[kx, row, y0 : y0 + RAD, :] -= sent.rows(at, RAD)
            xband[kx, row] = valid[kx] * xband[kx, row]
    for ky, message in enumerate((ylow, yhigh)):
        y0 = (ey - RAD) * ky
        for kx in range(2):
            for i in range(RAD):
                row = RAD * (1 - kx) + i
                at = RAD * ((nx - RAD) * kx + i)
                xband[kx, row, y0 : y0 + RAD, :] -= message.rows(at, RAD)
            for i in range(2 * RAD):
                xband[kx, i, y0 : y0 + RAD, :] = valid[2 + ky] * xband[kx, i, y0 : y0 + RAD, :]
        y0 = (BAND - RAD) * ky
        for i in range(nx - 2 * RAD):
            at = RAD * (RAD + i)
            inside = yband[ky, i, y0 : y0 + RAD, :] - message.rows(at, RAD)
            yband[ky, i, y0 : y0 + RAD, :] = valid[2 + ky] * inside

    stores = []
    for kx in range(2):
        for i in range(RAD):
            xout[kx, i] = xband[kx, RAD * (1 - kx) + i, RAD : RAD + ny, :].astype(jnp.bfloat16)
        stores.append(
            pltpu.make_async_copy(
                xout.at[kx], out_hbm.at[pl.ds((nx - RAD) * kx, RAD)], sems.at[kx]
            )
        )
    for ky in range(2):
        for i in range(nx - 2 * RAD):
            yout[ky, i] = yband[ky, i, RAD : RAD + SUB, :].astype(jnp.bfloat16)
        stores.append(
            pltpu.make_async_copy(
                yout.at[ky],
                out_hbm.at[pl.ds(RAD, nx - 2 * RAD), pl.ds((ny - SUB) * ky, SUB)],
                sems.at[2 + ky],
            )
        )
    for store in stores:
        store.start()
    for kx in range(2):
        for i in range(RAD):
            for j in range(ey // 8):
                rows = slice(8 * j, 8 * j + 8)
                pieces[(ex // 2 - RAD) * kx + i, 16 * j : 16 * j + 16, :] = packed(
                    xband[kx, 2 * i, rows, :], xband[kx, 2 * i + 1, rows, :]
                )
    for ky in range(2):
        rows = slice((BAND - 8) * ky, (BAND - 8) * ky + 8)
        at = 2 * (ey - 8) * ky
        for i in range(nx // 2 - RAD):
            pieces[RAD + i, at : at + 16, :] = packed(
                yband[ky, 2 * i, rows, :], yband[ky, 2 * i + 1, rows, :]
            )

    def x_edges(i, _):
        a, b = (i // cols_n) * (rows_n - 1), i % cols_n
        tile_gradient(own_atom(terms_ref, a * cols_n + b), pieces, prof_x, grad_ref, a, b)
        return 0

    def y_edges(i, _):
        a, b = i // 2 + 1, (i % 2) * (cols_n - 1)
        tile_gradient(own_atom(terms_ref, a * cols_n + b), pieces, prof_x, grad_ref, a, b)
        return 0

    lax.fori_loop(0, 2 * cols_n, x_edges, 0, unroll=8)
    lax.fori_loop(0, 2 * (rows_n - 2), y_edges, 0, unroll=4)
    for store in stores:
        store.wait()


def call(body, sizes, outs, in_specs, out_specs, scratch, cost, aliases=None):
    return pl.pallas_call(
        functools.partial(body, *sizes),
        out_shape=outs,
        in_specs=in_specs,
        out_specs=out_specs,
        scratch_shapes=scratch,
        input_output_aliases=aliases or {},
        cost_estimate=pl.CostEstimate(flops=cost, bytes_accessed=1 << 20, transcendentals=0),
        compiler_params=pltpu.CompilerParams(vmem_limit_bytes=VMEM_LIMIT),
    )


def local(atom_pos, b_factor, amplitude, counts, density_map):
    sizes = rows_n, cols_n = counts.shape
    nx, ny = rows_n * SUB, cols_n * SUB
    ex, ey = nx + 2 * RAD, ny + 2 * RAD
    f32, bf16 = jnp.float32, jnp.bfloat16
    shape = jax.ShapeDtypeStruct
    vmem = pl.BlockSpec(memory_space=pltpu.VMEM)
    hbm = pl.BlockSpec(memory_space=pltpu.HBM)
    pin = functools.partial(pltpu.with_memory_space_constraint, memory_space=pltpu.VMEM)
    own_scratch = [
        pltpu.SMEM(counts.shape, jnp.int32),
        pltpu.VMEM(atom_pos.shape, f32),
        pltpu.VMEM(b_factor.shape, f32),
        pltpu.VMEM(amplitude.shape, f32),
        pltpu.SemaphoreType.DMA((5,)),
    ]
    own = tuple(
        pltpu.with_memory_space_constraint(array, pltpu.HBM)
        for array in (counts, atom_pos, b_factor, amplitude)
    )
    density_map = pltpu.with_memory_space_constraint(density_map, pltpu.HBM)

    xsize, ysize = RAD * ny + FIELDS * cols_n, RAD * nx + BAND
    xlow, xhigh, first, second, found = call(
        message_kernel,
        sizes,
        (shape((xsize, CAP), f32),) * 2
        + (shape((ysize, CAP), f32),) * 2
        + (pltpu.VMEM((rows_n * cols_n, 8, CAP), f32),),
        [hbm] * 5,
        (vmem,) * 5,
        own_scratch
        + [
            pltpu.VMEM((2, RAD, ny, DEPTH), bf16),
            pltpu.VMEM((2, nx, SUB, DEPTH), bf16),
            pltpu.SemaphoreType.DMA((4,)),
        ],
        10**6,
    )(*own, density_map)
    from_first, from_second = swap(first, False), swap(second, True)
    from_xlow, from_xhigh = shift(xhigh, "bx", 1), shift(xlow, "bx", -1)

    bands = (
        pltpu.VMEM((2, 2 * RAD, ey, DEPTH), f32),
        pltpu.VMEM((2, nx - 2 * RAD, BAND, DEPTH), f32),
    )
    pieces = pltpu.VMEM((ex // 2, 2 * ey, 2 * DEPTH), bf16)
    residual, *kept, gradient = call(
        inner_kernel,
        sizes,
        (
            shape((nx, ny, DEPTH), bf16),
            pieces,
            *bands,
            shape((4, rows_n, cols_n, CAP), f32),
        ),
        [vmem, hbm],
        (hbm, vmem, vmem, vmem, vmem),
        [
            pltpu.VMEM((ex, ey, DEPTH), f32),
            pltpu.VMEM((nx, ny, DEPTH), bf16),
            pltpu.VMEM((nx, ny, DEPTH), bf16),
            pltpu.VMEM((3, TILE, CAP), f32),
            pltpu.SemaphoreType.DMA,
            pltpu.SemaphoreType.DMA((5,)),
        ],
        10**10,
    )(pin(found), density_map)
    kept_pieces, xband, yband = kept

    corners = call(
        corner_kernel,
        sizes,
        shape((4 * (RAD * RAD + FIELDS) + 4, CAP), f32),
        [vmem, vmem],
        vmem,
        [],
        10**5,
    )(from_xlow, from_xhigh)
    from_corners = swap(corners, False), swap(corners, True)

    messages = (from_xlow, from_xhigh, from_first, from_second)
    xband, yband = call(
        sides_kernel,
        sizes,
        bands,
        [vmem] * 6,
        (vmem, vmem),
        [],
        2 * 10**9,
        {4: 0, 5: 1},
    )(*messages, pin(xband), pin(yband))

    residual, gradient, *_ = call(
        outer_kernel,
        sizes,
        (
            shape((nx, ny, DEPTH), bf16),
            shape((4, rows_n, cols_n, CAP), f32),
            *bands,
            pieces,
        ),
        [vmem] * 11 + [hbm],
        (hbm, vmem, vmem, vmem, vmem),
        [
            pltpu.VMEM((2, RAD, ny, DEPTH), bf16),
            pltpu.VMEM((2, nx - 2 * RAD, SUB, DEPTH), bf16),
            pltpu.VMEM((3, TILE, CAP), f32),
            pltpu.SemaphoreType.DMA((4,)),
        ],
        10**10,
        {11: 0, 7: 2, 8: 3, 9: 4},
    )(
        pin(found), *messages, *from_corners,
        pin(xband), pin(yband), pin(kept_pieces), gradient, residual,
    )
    return residual, gradient


def solution(mesh):
    return jax.shard_map(
        local,
        mesh=mesh,
        in_specs=(
            P(None, "bx", "by", None),
            P("bx", "by", None),
            P("bx", "by", None),
            P("bx", "by"),
            P("bx", "by", None),
        ),
        out_specs=(P("bx", "by", None), P(None, "bx", "by", None)),
        check_vma=False,
    )
```

```python
import functools
import math

import jax
import jax.numpy as jnp
from jax import lax
from jax.experimental import pallas as pl
from jax.experimental.pallas import tpu as pltpu
from jax.sharding import PartitionSpec as P

SUB = 16
RAD = 4
TILE = 24
CAP = 128
DEPTH = 128
FIELDS = 5
BAND = 24

EIGHT_PI_SQ = 8.0 * math.pi**2
BLUR_VAR = 0.5
REACH_SQ = float(RAD * RAD)
VMEM_LIMIT = 18 << 20


def shift(block, axis, step):
    peers = lax.axis_size(axis)
    route = [(i, (i + step) % peers) for i in range(peers)]
    return lax.ppermute(block, axis, route)


def swap(block, odd):
    nx, ny = lax.axis_size("bx"), lax.axis_size("by")
    route = []
    for x in range(nx):
        for y in range(ny):
            to_x, to_y = x, (y ^ 1 if not odd else ((y + 1) ^ 1) - 1)
            if not 0 <= to_y < ny:
                to_x, to_y = x ^ 1, y
            route.append((x * ny + y, to_x * ny + to_y))
    return lax.ppermute(block, ("bx", "by"), route)


def is_even():
    return lax.axis_index("by") % 2 == 0


def valid_sides():
    found = []
    for axis in ("bx", "by"):
        at = lax.axis_index(axis)
        found += [at > 0, at < lax.axis_size(axis) - 1]
    return [jnp.where(side, 1.0, 0.0) for side in found]


class Picked:
    def __init__(self, flag, when_true, when_false):
        self.flag, self.refs = flag, (when_true, when_false)

    def rows(self, at, count):
        where = pl.ds(at, count)
        return jnp.where(self.flag, self.refs[0][where, :], self.refs[1][where, :])


class Plain:
    def __init__(self, ref):
        self.ref = ref

    def rows(self, at, count):
        return self.ref[pl.ds(at, count), :]


def split(value):
    high = value.astype(jnp.bfloat16)
    low = (value - high.astype(jnp.float32)).astype(jnp.bfloat16)
    return high, low


def base_profile(coordinate, sharpness, span, offset):
    grid = (lax.broadcasted_iota(jnp.int32, (span, CAP), 0) + offset).astype(jnp.float32)
    distance = grid - coordinate
    square = distance * distance
    falloff = jnp.maximum(1.0 - square * (1.0 / REACH_SQ), 0.0)
    damped = jnp.exp(-sharpness * square) * falloff
    return distance, square, falloff, damped


def value_only(coordinate, sharpness, span, offset):
    _, _, falloff, damped = base_profile(coordinate, sharpness, span, offset)
    return damped * falloff


def all_kinds(coordinate, sharpness, span, offset):
    distance, square, falloff, damped = base_profile(coordinate, sharpness, span, offset)
    value = damped * falloff
    slope = 2.0 * distance * (sharpness * value + (2.0 / REACH_SQ) * damped)
    width = -square * value
    return value, slope, width


def terms(x, y, z, b_factor):
    cx, cy, cz = x * float(SUB), y * float(SUB), z * float(DEPTH)
    return cx, cy, cz, 0.5 / (b_factor / EIGHT_PI_SQ + BLUR_VAR)


def fetch(pairs, sems):
    copies = [pltpu.make_async_copy(a, b, sems.at[i]) for i, (a, b) in enumerate(pairs)]
    for copy in copies:
        copy.start()
    return copies


def finish(copies):
    for copy in copies:
        copy.wait()


def masked(amplitude, count):
    slot = lax.broadcasted_iota(jnp.int32, (1, CAP), 1)
    return jnp.where(slot < count, amplitude, 0.0)


def own_atom(terms_ref, index):
    return tuple(terms_ref[index, k : k + 1, :] for k in range(FIELDS))


def sent_atom(message, start, stride, index, valid):
    row = [message.rows(start + k * stride + index, 1) for k in range(FIELDS)]
    return terms(*row[:4]) + (row[4] * valid,)


def rendered(atom, p0, p_n, j0, j_n):
    cx, cy, cz, sharp, weight = atom
    vx = value_only(cx, sharp, p_n, p0 - RAD) * weight
    vy = value_only(cy, sharp, 8 * j_n, 8 * j0 - RAD)
    z_hi, z_lo = split(value_only(cz, sharp, DEPTH, 0))
    weights = jnp.concatenate(
        [jnp.concatenate([z_hi, z_hi], 1), jnp.concatenate([z_lo, z_lo], 1)], 0
    )
    rows = []
    for p in range(p_n):
        for j in range(j_n):
            rows.append(vx[p : p + 1] * vy[8 * j : 8 * j + 8])
    plane_hi, plane_lo = split(jnp.concatenate(rows, 0))
    plane = jnp.concatenate([plane_hi, plane_lo], 1)
    both = lax.dot_general(
        plane, weights, (((1,), (1,)), ((), ())), preferred_element_type=jnp.float32
    )
    total = both[:, :DEPTH] + both[:, DEPTH:]
    return [total[8 * j_n * p : 8 * j_n * (p + 1)] for p in range(p_n)]


def packed(first, second):
    hi, lo = split(jnp.concatenate([first, second], 0))
    return jnp.concatenate([hi, lo], 1)


def tile_gradient(atom, pieces, prof_x, grad_ref, a, b):
    cx, cy, cz, sharp, weight = atom
    for k, kind in enumerate(all_kinds(cx, sharp, TILE, -RAD)):
        prof_x[k] = kind
    vy, sy, wy = all_kinds(cy, sharp, TILE, -RAD)
    vz, sz, wz = all_kinds(cz, sharp, DEPTH, 0)
    vz_hi, vz_lo = split(vz)
    sz_hi, sz_lo = split(sz)
    wz_hi = wz.astype(jnp.bfloat16)
    tile = pieces[pl.ds(8 * a, TILE // 2), pl.ds(pl.multiple_of(32 * b, 32), 2 * TILE), :]
    tile = tile.reshape(TILE * TILE, 2 * DEPTH)

    def project(rhs):
        return jnp.dot(tile, jnp.concatenate([rhs, rhs], 0), preferred_element_type=jnp.float32)

    proj_v = project(jnp.concatenate([vz_hi, vz_lo], 1))
    proj_s = project(jnp.concatenate([sz_hi, sz_lo], 1))
    proj_w = project(wz_hi)
    acc = [[jnp.zeros((8, CAP), jnp.float32) for _ in range(3)] for _ in range(4)]
    for p in range(TILE):
        vx = prof_x[0, p : p + 1, :]
        sx = prof_x[1, p : p + 1, :]
        wx = prof_x[2, p : p + 1, :]
        for j in range(3):
            at = ((p // 2) * 3 + j) * 16 + (p % 2) * 8
            base = proj_v[at : at + 8, :CAP] + proj_v[at : at + 8, CAP:]
            lift = proj_s[at : at + 8, :CAP] + proj_s[at : at + 8, CAP:]
            wide = proj_w[at : at + 8]
            acc[0][j] += base * vx
            acc[1][j] += base * sx
            acc[2][j] += lift * vx
            acc[3][j] += base * wx + wide * vx
    g_x = g_y = g_z = g_s = 0.0
    for j in range(3):
        at = slice(8 * j, 8 * j + 8)
        g_x += acc[1][j] * vy[at]
        g_y += acc[0][j] * sy[at]
        g_z += acc[2][j] * vy[at]
        g_s += acc[3][j] * vy[at] + acc[0][j] * wy[at]
    scale = -2.0 * sharp * sharp / EIGHT_PI_SQ
    for k, g in enumerate((g_x, g_y, g_z, g_s)):
        g = weight * jnp.sum(g, axis=0, keepdims=True)
        if k == 3:
            g = g * scale
        grad_ref[k, a, pl.ds(b, 1), :] = g


def message_kernel(
    rows_n, cols_n,
    counts_hbm, pos_hbm, bfac_hbm, amp_hbm, map_hbm,
    xlow_ref, xhigh_ref, first_ref, second_ref, terms_ref,
    counts_ref, pos_ref, bfac_ref, amp_ref, own_sems,
    xrim, yrim, sems,
):
    nx, ny = rows_n * SUB, cols_n * SUB
    held = (counts_ref, pos_ref, bfac_ref, amp_ref)
    fetched = fetch(zip((counts_hbm, pos_hbm, bfac_hbm, amp_hbm), held), own_sems)
    copies = []
    for k, at in enumerate((0, nx - RAD)):
        copies.append(pltpu.make_async_copy(map_hbm.at[pl.ds(at, RAD)], xrim.at[k], sems.at[k]))
    for k, at in enumerate((0, ny - SUB)):
        copies.append(
            pltpu.make_async_copy(map_hbm.at[:, pl.ds(at, SUB)], yrim.at[k], sems.at[2 + k])
        )
    for copy in copies:
        copy.start()

    def fields(a, b):
        found = [pos_ref[k, a, b : b + 1, :] for k in range(3)] + [bfac_ref[a, b : b + 1, :]]
        return found + [masked(amp_ref[a, b : b + 1, :], counts_ref[a, b])]

    def atoms(out, start, stride, index, a, b):
        for k, value in enumerate(fields(a, b)):
            out[start + k * stride + index : start + k * stride + index + 1, :] = value

    finish(fetched)
    for a in range(rows_n):
        found = terms(pos_ref[0, a], pos_ref[1, a], pos_ref[2, a], bfac_ref[a])
        for b in range(cols_n):
            row = slice(b, b + 1)
            weight = masked(amp_ref[a, row, :], counts_ref[a, b])
            terms_ref[a * cols_n + b, 0:FIELDS, :] = jnp.concatenate(
                [value[row] for value in found] + [weight], 0
            )
    for b in range(cols_n):
        atoms(xlow_ref, RAD * ny, cols_n, b, 0, b)
        atoms(xhigh_ref, RAD * ny, cols_n, b, rows_n - 1, b)
    even = is_even()

    def put(where, low, high):
        first_ref[where, :] = jnp.where(even, high, low)
        second_ref[where, :] = jnp.where(even, low, high)

    for out in (first_ref, second_ref):
        out[nx * RAD :, :] = jnp.zeros((BAND, CAP), jnp.float32)
    for a in range(rows_n):
        low, high = fields(a, 0), fields(a, cols_n - 1)
        for k in range(FIELDS):
            at = RAD * nx + k * rows_n + a
            put(slice(at, at + 1), low[k], high[k])
    for copy in copies:
        copy.wait()
    for k, out in enumerate((xlow_ref, xhigh_ref)):
        for i in range(RAD):
            out[ny * i : ny * (i + 1), :] = xrim[k, i].astype(jnp.float32)
    for i in range(nx):
        put(
            slice(RAD * i, RAD * (i + 1)),
            yrim[0, i].astype(jnp.float32)[:RAD],
            yrim[1, i].astype(jnp.float32)[SUB - RAD :],
        )


def inner_kernel(
    rows_n, cols_n,
    terms_ref, map_hbm,
    out_hbm, pieces, xband, yband, grad_ref,
    field, map_v, out_v, prof_x, in_sem, out_sems,
):
    nx, ny = rows_n * SUB, cols_n * SUB
    ex, ey = nx + 2 * RAD, ny + 2 * RAD
    load = pltpu.make_async_copy(map_hbm, map_v, in_sem)
    load.start()

    for i in range(2 * RAD):
        field[i] = jnp.zeros((ey, DEPTH), jnp.float32)
    for i in range(2 * RAD, ex):
        field[i, 0 : 2 * RAD, :] = jnp.zeros((2 * RAD, DEPTH), jnp.float32)

    def own(i, _):
        a, b = i // cols_n, i % cols_n
        y0 = pl.multiple_of(SUB * b, SUB)
        y1 = pl.multiple_of(SUB * b + 2 * RAD, 2 * RAD)
        for p, row in enumerate(rendered(own_atom(terms_ref, i), 0, TILE, 0, 3)):
            if p < 2 * RAD:
                field[SUB * a + p, pl.ds(y0, TILE), :] += row
            else:
                field[SUB * a + p, pl.ds(y0, 2 * RAD), :] += row[: 2 * RAD]
                field[SUB * a + p, pl.ds(y1, SUB), :] = row[2 * RAD :]
        return 0

    lax.fori_loop(0, rows_n * cols_n, own, 0, unroll=8)
    load.wait()

    def brick(i, _):
        inside = field[i + RAD, RAD : RAD + ny, :] - map_v[i].astype(jnp.float32)
        field[i + RAD, RAD : RAD + ny, :] = inside
        out_v[i] = inside.astype(jnp.bfloat16)
        return 0

    lax.fori_loop(0, nx, brick, 0, unroll=8)
    rest = pl.ds(2 * RAD, nx - 2 * RAD)
    pairs = [(out_v, out_hbm)]
    for k in range(2):
        pairs.append((field.at[pl.ds((ex - 2 * RAD) * k, 2 * RAD)], xband.at[k]))
        pairs.append((field.at[rest, pl.ds((ey - BAND) * k, BAND)], yband.at[k]))
    stores = fetch(pairs, out_sems)

    def pack(i, _):
        for j in range(ey // 8):
            rows = pl.ds(8 * j, 8)
            pieces[i, 16 * j : 16 * j + 16, :] = packed(field[2 * i, rows, :], field[2 * i + 1, rows, :])
        return 0

    lax.fori_loop(RAD, ex // 2 - RAD, pack, 0, unroll=4)
    def gradient(i, _):
        a, b = i // (cols_n - 2) + 1, i % (cols_n - 2) + 1
        tile_gradient(own_atom(terms_ref, a * cols_n + b), pieces, prof_x, grad_ref, a, b)
        return 0

    lax.fori_loop(0, (rows_n - 2) * (cols_n - 2), gradient, 0, unroll=12)
    finish(stores)


def corner_kernel(rows_n, cols_n, first_ref, second_ref, up_ref, down_ref):
    nx = rows_n * SUB
    even = is_even()
    ylow, yhigh = Picked(even, second_ref, first_ref), Picked(even, first_ref, second_ref)
    block = RAD * RAD
    for out, x0, a in ((up_ref, nx - RAD, rows_n - 1), (down_ref, 0, 0)):
        for ky, message in enumerate((ylow, yhigh)):
            at = (block + FIELDS) * ky
            out[at : at + block, :] = message.rows(RAD * x0, block)
            for k in range(FIELDS):
                row = at + block + k
                out[row : row + 1, :] = message.rows(RAD * nx + k * rows_n + a, 1)
        at = 2 * (block + FIELDS)
        out[at:, :] = jnp.zeros((out.shape[0] - at, CAP), jnp.float32)


def sides_kernel(
    rows_n, cols_n,
    xlow_ref, xhigh_ref, first_ref, second_ref, xband_in, yband_in,
    xband, yband,
):
    nx, ny = rows_n * SUB, cols_n * SUB
    ex, ey = nx + 2 * RAD, ny + 2 * RAD
    even, valid = is_even(), valid_sides()
    ylow, yhigh = Picked(even, second_ref, first_ref), Picked(even, first_ref, second_ref)

    def x_side(b, _):
        y0 = pl.multiple_of(SUB * b, SUB)
        for k, (message, p0) in enumerate(((Plain(xlow_ref), SUB), (Plain(xhigh_ref), 0))):
            atom = sent_atom(message, RAD * ny, cols_n, b, valid[k])
            for p, row in enumerate(rendered(atom, p0, 2 * RAD, 0, 3)):
                xband[k, p, pl.ds(y0, TILE), :] += row
        return 0

    lax.fori_loop(0, cols_n, x_side, 0, unroll=4)
    for a in range(rows_n):
        for k, (message, j0, y0) in enumerate(((ylow, 2, 0), (yhigh, 0, ey - 8))):
            atom = sent_atom(message, RAD * nx, rows_n, a, valid[2 + k])
            for p, row in enumerate(rendered(atom, 0, TILE, j0, 1)):
                x = SUB * a + p
                if x < 2 * RAD:
                    xband[0, x, y0 : y0 + 8, :] += row
                elif x >= ex - 2 * RAD:
                    xband[1, x - (ex - 2 * RAD), y0 : y0 + 8, :] += row
                else:
                    yband[k, x - 2 * RAD, (BAND - 8) * k : (BAND - 8) * k + 8, :] += row


def outer_kernel(
    rows_n, cols_n,
    terms_ref, xlow_ref, xhigh_ref, first_ref, second_ref, clow_ref, chigh_ref,
    xband_in, yband_in, pieces_in, grad_in, out_in,
    out_hbm, grad_ref, xband, yband, pieces,
    xout, yout, prof_x, sems,
):
    nx, ny = rows_n * SUB, cols_n * SUB
    ex, ey = nx + 2 * RAD, ny + 2 * RAD
    grad_ref[...] = grad_in[...]
    corner = RAD * RAD + FIELDS
    even, valid = is_even(), valid_sides()
    ylow, yhigh = Picked(even, second_ref, first_ref), Picked(even, first_ref, second_ref)
    sent = Plain(clow_ref), Plain(chigh_ref)
    for ky, (j0, y0) in enumerate(((2, 0), (0, ey - 8))):
        for kx, p0 in enumerate((SUB, 0)):
            ok = valid[kx] * valid[2 + ky]
            atom = sent_atom(sent[kx], corner * ky + RAD * RAD, 1, 0, ok)
            for p, row in enumerate(rendered(atom, p0, 2 * RAD, j0, 1)):
                xband[kx, p, y0 : y0 + 8, :] += row
    for kx, message in enumerate((xlow_ref, xhigh_ref)):
        for i in range(RAD):
            row = RAD * kx + i
            xband[kx, row, RAD : RAD + ny, :] -= message[ny * i : ny * (i + 1), :]
            for ky in range(2):
                y0 = (ey - RAD) * ky
                xband[kx, row, y0 : y0 + RAD, :] -= sent[kx].rows(corner * ky + RAD * i, RAD)
            xband[kx, row] = valid[kx] * xband[kx, row]
    for ky, message in enumerate((ylow, yhigh)):
        y0 = (ey - RAD) * ky
        for kx in range(2):
            for i in range(RAD):
                row = RAD * (1 - kx) + i
                at = RAD * ((nx - RAD) * kx + i)
                xband[kx, row, y0 : y0 + RAD, :] -= message.rows(at, RAD)
            for i in range(2 * RAD):
                xband[kx, i, y0 : y0 + RAD, :] = valid[2 + ky] * xband[kx, i, y0 : y0 + RAD, :]
        y0 = (BAND - RAD) * ky
        for i in range(nx - 2 * RAD):
            at = RAD * (RAD + i)
            inside = yband[ky, i, y0 : y0 + RAD, :] - message.rows(at, RAD)
            yband[ky, i, y0 : y0 + RAD, :] = valid[2 + ky] * inside

    stores = []
    for kx in range(2):
        for i in range(RAD):
            xout[kx, i] = xband[kx, RAD * (1 - kx) + i, RAD : RAD + ny, :].astype(jnp.bfloat16)
        stores.append(
            pltpu.make_async_copy(
                xout.at[kx], out_hbm.at[pl.ds((nx - RAD) * kx, RAD)], sems.at[kx]
            )
        )
    for ky in range(2):
        for i in range(nx - 2 * RAD):
            yout[ky, i] = yband[ky, i, RAD : RAD + SUB, :].astype(jnp.bfloat16)
        stores.append(
            pltpu.make_async_copy(
                yout.at[ky],
                out_hbm.at[pl.ds(RAD, nx - 2 * RAD), pl.ds((ny - SUB) * ky, SUB)],
                sems.at[2 + ky],
            )
        )
    for store in stores:
        store.start()
    for kx in range(2):
        for i in range(RAD):
            for j in range(ey // 8):
                rows = slice(8 * j, 8 * j + 8)
                pieces[(ex // 2 - RAD) * kx + i, 16 * j : 16 * j + 16, :] = packed(
                    xband[kx, 2 * i, rows, :], xband[kx, 2 * i + 1, rows, :]
                )
    for ky in range(2):
        rows = slice((BAND - 8) * ky, (BAND - 8) * ky + 8)
        at = 2 * (ey - 8) * ky
        for i in range(nx // 2 - RAD):
            pieces[RAD + i, at : at + 16, :] = packed(
                yband[ky, 2 * i, rows, :], yband[ky, 2 * i + 1, rows, :]
            )

    def edges(i, _):
        k = jnp.maximum(i - 2 * cols_n, 0)
        side = i < 2 * cols_n
        a = jnp.where(side, (i // cols_n) * (rows_n - 1), k // 2 + 1)
        b = jnp.where(side, i % cols_n, (k % 2) * (cols_n - 1))
        tile_gradient(own_atom(terms_ref, a * cols_n + b), pieces, prof_x, grad_ref, a, b)
        return 0

    lax.fori_loop(0, 2 * cols_n + 2 * (rows_n - 2), edges, 0, unroll=10)
    for store in stores:
        store.wait()


def call(body, sizes, outs, in_specs, out_specs, scratch, cost, aliases=None):
    return pl.pallas_call(
        functools.partial(body, *sizes),
        out_shape=outs,
        in_specs=in_specs,
        out_specs=out_specs,
        scratch_shapes=scratch,
        input_output_aliases=aliases or {},
        cost_estimate=pl.CostEstimate(flops=cost, bytes_accessed=1 << 20, transcendentals=0),
        compiler_params=pltpu.CompilerParams(vmem_limit_bytes=VMEM_LIMIT),
    )


def local(atom_pos, b_factor, amplitude, counts, density_map):
    sizes = rows_n, cols_n = counts.shape
    nx, ny = rows_n * SUB, cols_n * SUB
    ex, ey = nx + 2 * RAD, ny + 2 * RAD
    f32, bf16 = jnp.float32, jnp.bfloat16
    shape = jax.ShapeDtypeStruct
    vmem = pl.BlockSpec(memory_space=pltpu.VMEM)
    hbm = pl.BlockSpec(memory_space=pltpu.HBM)
    pin = functools.partial(pltpu.with_memory_space_constraint, memory_space=pltpu.VMEM)
    own_scratch = [
        pltpu.SMEM(counts.shape, jnp.int32),
        pltpu.VMEM(atom_pos.shape, f32),
        pltpu.VMEM(b_factor.shape, f32),
        pltpu.VMEM(amplitude.shape, f32),
        pltpu.SemaphoreType.DMA((5,)),
    ]
    own = tuple(
        pltpu.with_memory_space_constraint(array, pltpu.HBM)
        for array in (counts, atom_pos, b_factor, amplitude)
    )
    density_map = pltpu.with_memory_space_constraint(density_map, pltpu.HBM)

    xsize, ysize = RAD * ny + FIELDS * cols_n, RAD * nx + BAND
    xlow, xhigh, first, second, found = call(
        message_kernel,
        sizes,
        (shape((xsize, CAP), f32),) * 2
        + (shape((ysize, CAP), f32),) * 2
        + (pltpu.VMEM((rows_n * cols_n, 8, CAP), f32),),
        [hbm] * 5,
        (vmem,) * 5,
        own_scratch
        + [
            pltpu.VMEM((2, RAD, ny, DEPTH), bf16),
            pltpu.VMEM((2, nx, SUB, DEPTH), bf16),
            pltpu.SemaphoreType.DMA((4,)),
        ],
        10**6,
    )(*own, density_map)
    from_first, from_second = swap(first, False), swap(second, True)
    from_xlow, from_xhigh = shift(xhigh, "bx", 1), shift(xlow, "bx", -1)

    bands = (
        pltpu.VMEM((2, 2 * RAD, ey, DEPTH), f32),
        pltpu.VMEM((2, nx - 2 * RAD, BAND, DEPTH), f32),
    )
    pieces = pltpu.VMEM((ex // 2, 2 * ey, 2 * DEPTH), bf16)
    residual, *kept, gradient = call(
        inner_kernel,
        sizes,
        (
            shape((nx, ny, DEPTH), bf16),
            pieces,
            *bands,
            shape((4, rows_n, cols_n, CAP), f32),
        ),
        [vmem, hbm],
        (hbm, vmem, vmem, vmem, vmem),
        [
            pltpu.VMEM((ex, ey, DEPTH), f32),
            pltpu.VMEM((nx, ny, DEPTH), bf16),
            pltpu.VMEM((nx, ny, DEPTH), bf16),
            pltpu.VMEM((3, TILE, CAP), f32),
            pltpu.SemaphoreType.DMA,
            pltpu.SemaphoreType.DMA((5,)),
        ],
        10**10,
    )(pin(found), density_map)
    kept_pieces, xband, yband = kept

    edge = shape((2 * (RAD * RAD + FIELDS) + 6, CAP), f32)
    up, down = call(
        corner_kernel, sizes, (edge, edge), [vmem, vmem], (vmem, vmem), [], 10**5
    )(from_first, from_second)
    from_corners = shift(up, "bx", 1), shift(down, "bx", -1)

    messages = (from_xlow, from_xhigh, from_first, from_second)
    xband, yband = call(
        sides_kernel,
        sizes,
        bands,
        [vmem] * 6,
        (vmem, vmem),
        [],
        2 * 10**9,
        {4: 0, 5: 1},
    )(*messages, pin(xband), pin(yband))

    residual, gradient, *_ = call(
        outer_kernel,
        sizes,
        (
            shape((nx, ny, DEPTH), bf16),
            shape((4, rows_n, cols_n, CAP), f32),
            *bands,
            pieces,
        ),
        [vmem] * 11 + [hbm],
        (hbm, vmem, vmem, vmem, vmem),
        [
            pltpu.VMEM((2, RAD, ny, DEPTH), bf16),
            pltpu.VMEM((2, nx - 2 * RAD, SUB, DEPTH), bf16),
            pltpu.VMEM((3, TILE, CAP), f32),
            pltpu.SemaphoreType.DMA((4,)),
        ],
        10**10,
        {11: 0, 7: 2, 8: 3, 9: 4},
    )(
        pin(found), *messages, *from_corners,
        pin(xband), pin(yband), pin(kept_pieces), gradient, residual,
    )
    return residual, gradient


def solution(mesh):
    return jax.shard_map(
        local,
        mesh=mesh,
        in_specs=(
            P(None, "bx", "by", None),
            P("bx", "by", None),
            P("bx", "by", None),
            P("bx", "by"),
            P("bx", "by", None),
        ),
        out_specs=(P("bx", "by", None), P(None, "bx", "by", None)),
        check_vma=False,
    )
```

```python
import functools
import math

import jax
import jax.numpy as jnp
from jax import lax
from jax.experimental import pallas as pl
from jax.experimental.pallas import tpu as pltpu
from jax.sharding import PartitionSpec as P

SUB = 16
RAD = 4
TILE = 24
CAP = 128
DEPTH = 128
FIELDS = 5
BAND = 24

EIGHT_PI_SQ = 8.0 * math.pi**2
BLUR_VAR = 0.5
REACH_SQ = float(RAD * RAD)
LOG2_E = math.log2(math.e)
VMEM_LIMIT = 18 << 20


def shift(block, axis, step):
    peers = lax.axis_size(axis)
    route = [(i, (i + step) % peers) for i in range(peers)]
    return lax.ppermute(block, axis, route)


def swap(block, odd):
    nx, ny = lax.axis_size("bx"), lax.axis_size("by")
    route = []
    for x in range(nx):
        for y in range(ny):
            to_x, to_y = x, (y ^ 1 if not odd else ((y + 1) ^ 1) - 1)
            if not 0 <= to_y < ny:
                to_x, to_y = x ^ 1, y
            route.append((x * ny + y, to_x * ny + to_y))
    return lax.ppermute(block, ("bx", "by"), route)


def is_even():
    return lax.axis_index("by") % 2 == 0


def valid_sides():
    found = []
    for axis in ("bx", "by"):
        at = lax.axis_index(axis)
        found += [at > 0, at < lax.axis_size(axis) - 1]
    return [jnp.where(side, 1.0, 0.0) for side in found]


class Picked:
    def __init__(self, flag, when_true, when_false):
        self.flag, self.refs = flag, (when_true, when_false)

    def rows(self, at, count):
        where = pl.ds(at, count)
        return jnp.where(self.flag, self.refs[0][where, :], self.refs[1][where, :])


class Plain:
    def __init__(self, ref):
        self.ref = ref

    def rows(self, at, count):
        return self.ref[pl.ds(at, count), :]


def split(value):
    high = value.astype(jnp.bfloat16)
    low = (value - high.astype(jnp.float32)).astype(jnp.bfloat16)
    return high, low


def grid_of(span):
    return lax.broadcasted_iota(jnp.int32, (span, CAP), 0).astype(jnp.float32)


def base_profile(coordinate, sharpness, grid):
    distance = grid - coordinate
    square = distance * distance
    falloff = jnp.maximum(1.0 - square * (1.0 / REACH_SQ), 0.0)
    damped = jnp.exp2(square * (sharpness * (-LOG2_E))) * falloff
    return distance, square, falloff, damped


def value_only(coordinate, sharpness, grid):
    _, _, falloff, damped = base_profile(coordinate, sharpness, grid)
    return damped * falloff


def all_kinds(coordinate, sharpness, grid):
    distance, square, falloff, damped = base_profile(coordinate, sharpness, grid)
    value = damped * falloff
    slope = distance * (2.0 * sharpness * value + (4.0 / REACH_SQ) * damped)
    width = -square * value
    return value, slope, width


def terms(x, y, z, b_factor):
    cx, cy, cz = x * float(SUB), y * float(SUB), z * float(DEPTH)
    return cx, cy, cz, 0.5 / (b_factor / EIGHT_PI_SQ + BLUR_VAR)


def fetch(pairs, sems):
    copies = [pltpu.make_async_copy(a, b, sems.at[i]) for i, (a, b) in enumerate(pairs)]
    for copy in copies:
        copy.start()
    return copies


def finish(copies):
    for copy in copies:
        copy.wait()


def masked(amplitude, count):
    slot = lax.broadcasted_iota(jnp.int32, (1, CAP), 1)
    return jnp.where(slot < count, amplitude, 0.0)


def own_atom(terms_ref, index):
    return tuple(terms_ref[index, k : k + 1, :] for k in range(FIELDS))


def sent_atom(message, start, stride, index, valid):
    row = [message.rows(start + k * stride + index, 1) for k in range(FIELDS)]
    return terms(*row[:4]) + (row[4] * valid,)


def rendered(atom, z_parts, p0, p_n, j0, j_n):
    cx, cy, cz, sharp, weight = atom
    grid = grid_of(TILE) - float(RAD)
    vx = value_only(cx, sharp, grid[p0 : p0 + p_n]) * weight
    vy = value_only(cy, sharp, grid[8 * j0 : 8 * j0 + 8 * j_n])
    z_hi, z_lo = z_parts
    weights = jnp.concatenate(
        [jnp.concatenate([z_hi, z_hi], 1), jnp.concatenate([z_lo, z_lo], 1)], 0
    )
    out = []
    step = TILE // 2 if p_n == TILE else p_n
    for start in range(0, p_n, step):
        rows = []
        for p in range(start, start + step):
            for j in range(j_n):
                rows.append(vx[p : p + 1] * vy[8 * j : 8 * j + 8])
        plane_hi, plane_lo = split(jnp.concatenate(rows, 0))
        plane = jnp.concatenate([plane_hi, plane_lo], 1)
        both = lax.dot_general(
            plane, weights, (((1,), (1,)), ((), ())), preferred_element_type=jnp.float32
        )
        total = both[:, :DEPTH] + both[:, DEPTH:]
        out += [total[8 * j_n * p : 8 * j_n * (p + 1)] for p in range(step)]
    return out


def z_value(atom, grid):
    return split(value_only(atom[2], atom[3], grid))


def packed(first, second):
    hi, lo = split(jnp.concatenate([first, second], 0))
    return jnp.concatenate([hi, lo], 1)


def tile_gradient(atom, z_grid, pieces, prof_x, grad_ref, a, b):
    cx, cy, cz, sharp, weight = atom
    grid = grid_of(TILE) - float(RAD)
    for k, kind in enumerate(all_kinds(cx, sharp, grid)):
        prof_x[k] = kind
    vy, sy, wy = all_kinds(cy, sharp, grid)
    vz, sz, wz = all_kinds(cz, sharp, z_grid)
    vz_hi, vz_lo = split(vz)
    sz_hi, sz_lo = split(sz)
    wz_hi = wz.astype(jnp.bfloat16)
    tile = pieces[pl.ds(8 * a, TILE // 2), pl.ds(pl.multiple_of(32 * b, 32), 2 * TILE), :]
    tile = tile.reshape(TILE * TILE, 2 * DEPTH)

    def project(rhs):
        return jnp.dot(tile, jnp.concatenate([rhs, rhs], 0), preferred_element_type=jnp.float32)

    proj_v = project(jnp.concatenate([vz_hi, vz_lo], 1))
    proj_s = project(jnp.concatenate([sz_hi, sz_lo], 1))
    proj_w = project(wz_hi)
    acc = [[jnp.zeros((8, CAP), jnp.float32) for _ in range(3)] for _ in range(4)]
    for p in range(TILE):
        vx = prof_x[0, p : p + 1, :]
        sx = prof_x[1, p : p + 1, :]
        wx = prof_x[2, p : p + 1, :]
        for j in range(3):
            at = ((p // 2) * 3 + j) * 16 + (p % 2) * 8
            base = proj_v[at : at + 8, :CAP] + proj_v[at : at + 8, CAP:]
            lift = proj_s[at : at + 8, :CAP] + proj_s[at : at + 8, CAP:]
            wide = proj_w[at : at + 8]
            acc[0][j] += base * vx
            acc[1][j] += base * sx
            acc[2][j] += lift * vx
            acc[3][j] += base * wx + wide * vx
    g_x = g_y = g_z = g_s = 0.0
    for j in range(3):
        at = slice(8 * j, 8 * j + 8)
        g_x += acc[1][j] * vy[at]
        g_y += acc[0][j] * sy[at]
        g_z += acc[2][j] * vy[at]
        g_s += acc[3][j] * vy[at] + acc[0][j] * wy[at]
    scale = -2.0 * sharp * sharp / EIGHT_PI_SQ
    for k, g in enumerate((g_x, g_y, g_z, g_s)):
        g = weight * jnp.sum(g, axis=0, keepdims=True)
        if k == 3:
            g = g * scale
        grad_ref[k, a, pl.ds(b, 1), :] = g


def message_kernel(
    rows_n, cols_n,
    counts_hbm, pos_hbm, bfac_hbm, amp_hbm, map_hbm,
    xlow_ref, xhigh_ref, first_ref, second_ref, terms_ref,
    counts_ref, pos_ref, bfac_ref, amp_ref, own_sems,
    xrim, yrim, sems,
):
    nx, ny = rows_n * SUB, cols_n * SUB
    held = (counts_ref, pos_ref, bfac_ref, amp_ref)
    fetched = fetch(zip((counts_hbm, pos_hbm, bfac_hbm, amp_hbm), held), own_sems)
    copies = []
    for k, at in enumerate((0, nx - RAD)):
        copies.append(pltpu.make_async_copy(map_hbm.at[pl.ds(at, RAD)], xrim.at[k], sems.at[k]))
    for k, at in enumerate((0, ny - 2 * RAD)):
        copies.append(
            pltpu.make_async_copy(map_hbm.at[:, pl.ds(at, 2 * RAD)], yrim.at[k], sems.at[2 + k])
        )
    for copy in copies:
        copy.start()

    def fields(a, b):
        found = [pos_ref[k, a, b : b + 1, :] for k in range(3)] + [bfac_ref[a, b : b + 1, :]]
        return found + [masked(amp_ref[a, b : b + 1, :], counts_ref[a, b])]

    def atoms(out, start, stride, index, a, b):
        for k, value in enumerate(fields(a, b)):
            out[start + k * stride + index : start + k * stride + index + 1, :] = value

    finish(fetched)
    for a in range(rows_n):
        found = terms(pos_ref[0, a], pos_ref[1, a], pos_ref[2, a], bfac_ref[a])
        for b in range(cols_n):
            row = slice(b, b + 1)
            weight = masked(amp_ref[a, row, :], counts_ref[a, b])
            terms_ref[a * cols_n + b, 0:FIELDS, :] = jnp.concatenate(
                [value[row] for value in found] + [weight], 0
            )
    for b in range(cols_n):
        atoms(xlow_ref, RAD * ny, cols_n, b, 0, b)
        atoms(xhigh_ref, RAD * ny, cols_n, b, rows_n - 1, b)
    even = is_even()

    def put(where, low, high):
        first_ref[where, :] = jnp.where(even, high, low)
        second_ref[where, :] = jnp.where(even, low, high)

    for out in (first_ref, second_ref):
        out[nx * RAD :, :] = jnp.zeros((BAND, CAP), jnp.float32)
    for a in range(rows_n):
        low, high = fields(a, 0), fields(a, cols_n - 1)
        for k in range(FIELDS):
            at = RAD * nx + k * rows_n + a
            put(slice(at, at + 1), low[k], high[k])
    for copy in copies:
        copy.wait()
    for k, out in enumerate((xlow_ref, xhigh_ref)):
        for i in range(RAD):
            out[ny * i : ny * (i + 1), :] = xrim[k, i].astype(jnp.float32)
    for i in range(nx):
        put(
            slice(RAD * i, RAD * (i + 1)),
            yrim[0, i].astype(jnp.float32)[:RAD],
            yrim[1, i].astype(jnp.float32)[RAD:],
        )


def inner_kernel(
    rows_n, cols_n,
    terms_ref, map_hbm,
    out_hbm, pieces, xband, yband, grad_ref,
    field, map_v, out_v, prof_x, in_sem, out_sems,
):
    nx, ny = rows_n * SUB, cols_n * SUB
    ex, ey = nx + 2 * RAD, ny + 2 * RAD
    load = pltpu.make_async_copy(map_hbm, map_v, in_sem)
    load.start()

    for i in range(2 * RAD):
        field[i] = jnp.zeros((ey, DEPTH), jnp.float32)
    for i in range(2 * RAD, ex):
        field[i, 0 : 2 * RAD, :] = jnp.zeros((2 * RAD, DEPTH), jnp.float32)

    grid = grid_of(DEPTH)

    def own(i, _):
        a, b = i // cols_n, i % cols_n
        y0 = pl.multiple_of(SUB * b, SUB)
        y1 = pl.multiple_of(SUB * b + 2 * RAD, 2 * RAD)
        atom = own_atom(terms_ref, i)
        for p, row in enumerate(rendered(atom, z_value(atom, grid), 0, TILE, 0, 3)):
            if p < 2 * RAD:
                field[SUB * a + p, pl.ds(y0, TILE), :] += row
            else:
                field[SUB * a + p, pl.ds(y0, 2 * RAD), :] += row[: 2 * RAD]
                field[SUB * a + p, pl.ds(y1, SUB), :] = row[2 * RAD :]
        return 0

    lax.fori_loop(0, rows_n * cols_n, own, 0, unroll=16)
    load.wait()

    def brick(i, _):
        inside = field[i + RAD, RAD : RAD + ny, :] - map_v[i].astype(jnp.float32)
        field[i + RAD, RAD : RAD + ny, :] = inside
        out_v[i] = inside.astype(jnp.bfloat16)
        return 0

    lax.fori_loop(0, nx, brick, 0, unroll=8)
    rest = pl.ds(2 * RAD, nx - 2 * RAD)
    pairs = [(out_v, out_hbm)]
    for k in range(2):
        pairs.append((field.at[pl.ds((ex - 2 * RAD) * k, 2 * RAD)], xband.at[k]))
        pairs.append((field.at[rest, pl.ds((ey - BAND) * k, BAND)], yband.at[k]))
    stores = fetch(pairs, out_sems)

    def pack(i, _):
        for j in range(ey // 8):
            rows = pl.ds(8 * j, 8)
            pieces[i, 16 * j : 16 * j + 16, :] = packed(field[2 * i, rows, :], field[2 * i + 1, rows, :])
        return 0

    lax.fori_loop(RAD, ex // 2 - RAD, pack, 0, unroll=4)
    def gradient(i, _):
        a, b = i // (cols_n - 2) + 1, i % (cols_n - 2) + 1
        tile_gradient(own_atom(terms_ref, a * cols_n + b), grid, pieces, prof_x, grad_ref, a, b)
        return 0

    lax.fori_loop(0, (rows_n - 2) * (cols_n - 2), gradient, 0, unroll=12)
    finish(stores)


def corner_kernel(rows_n, cols_n, first_ref, second_ref, up_ref, down_ref):
    nx = rows_n * SUB
    even = is_even()
    ylow, yhigh = Picked(even, second_ref, first_ref), Picked(even, first_ref, second_ref)
    block = RAD * RAD
    for out, x0, a in ((up_ref, nx - RAD, rows_n - 1), (down_ref, 0, 0)):
        for ky, message in enumerate((ylow, yhigh)):
            at = (block + FIELDS) * ky
            out[at : at + block, :] = message.rows(RAD * x0, block)
            for k in range(FIELDS):
                row = at + block + k
                out[row : row + 1, :] = message.rows(RAD * nx + k * rows_n + a, 1)
        at = 2 * (block + FIELDS)
        out[at:, :] = jnp.zeros((out.shape[0] - at, CAP), jnp.float32)


def sides_kernel(
    rows_n, cols_n,
    xlow_ref, xhigh_ref, first_ref, second_ref, xband_in, yband_in,
    xband, yband,
):
    nx, ny = rows_n * SUB, cols_n * SUB
    ex, ey = nx + 2 * RAD, ny + 2 * RAD
    even, valid = is_even(), valid_sides()
    ylow, yhigh = Picked(even, second_ref, first_ref), Picked(even, first_ref, second_ref)
    grid = grid_of(DEPTH)

    def x_side(b, _):
        y0 = pl.multiple_of(SUB * b, SUB)
        for k, (message, p0) in enumerate(((Plain(xlow_ref), SUB), (Plain(xhigh_ref), 0))):
            atom = sent_atom(message, RAD * ny, cols_n, b, valid[k])
            for p, row in enumerate(rendered(atom, z_value(atom, grid), p0, 2 * RAD, 0, 3)):
                xband[k, p, pl.ds(y0, TILE), :] += row
        return 0

    lax.fori_loop(0, cols_n, x_side, 0, unroll=4)
    for a in range(rows_n):
        for k, (message, j0, y0) in enumerate(((ylow, 2, 0), (yhigh, 0, ey - 8))):
            atom = sent_atom(message, RAD * nx, rows_n, a, valid[2 + k])
            for p, row in enumerate(rendered(atom, z_value(atom, grid), 0, TILE, j0, 1)):
                x = SUB * a + p
                if x < 2 * RAD:
                    xband[0, x, y0 : y0 + 8, :] += row
                elif x >= ex - 2 * RAD:
                    xband[1, x - (ex - 2 * RAD), y0 : y0 + 8, :] += row
                else:
                    yband[k, x - 2 * RAD, (BAND - 8) * k : (BAND - 8) * k + 8, :] += row


def outer_kernel(
    rows_n, cols_n,
    terms_ref, xlow_ref, xhigh_ref, first_ref, second_ref, clow_ref, chigh_ref,
    xband_in, yband_in, pieces_in, grad_in, out_in,
    out_hbm, grad_ref, xband, yband, pieces,
    xout, yout, prof_x, sems,
):
    nx, ny = rows_n * SUB, cols_n * SUB
    ex, ey = nx + 2 * RAD, ny + 2 * RAD
    grad_ref[...] = grad_in[...]
    corner = RAD * RAD + FIELDS
    even, valid = is_even(), valid_sides()
    ylow, yhigh = Picked(even, second_ref, first_ref), Picked(even, first_ref, second_ref)
    sent = Plain(clow_ref), Plain(chigh_ref)
    grid = grid_of(DEPTH)
    for ky, (j0, y0) in enumerate(((2, 0), (0, ey - 8))):
        for kx, p0 in enumerate((SUB, 0)):
            ok = valid[kx] * valid[2 + ky]
            atom = sent_atom(sent[kx], corner * ky + RAD * RAD, 1, 0, ok)
            for p, row in enumerate(rendered(atom, z_value(atom, grid), p0, 2 * RAD, j0, 1)):
                xband[kx, p, y0 : y0 + 8, :] += row
    for kx, message in enumerate((xlow_ref, xhigh_ref)):
        for i in range(RAD):
            row = RAD * kx + i
            xband[kx, row, RAD : RAD + ny, :] -= message[ny * i : ny * (i + 1), :]
            for ky in range(2):
                y0 = (ey - RAD) * ky
                xband[kx, row, y0 : y0 + RAD, :] -= sent[kx].rows(corner * ky + RAD * i, RAD)
            xband[kx, row] = valid[kx] * xband[kx, row]
    for ky, message in enumerate((ylow, yhigh)):
        y0 = (ey - RAD) * ky
        for kx in range(2):
            for i in range(RAD):
                row = RAD * (1 - kx) + i
                at = RAD * ((nx - RAD) * kx + i)
                xband[kx, row, y0 : y0 + RAD, :] -= message.rows(at, RAD)
            for i in range(2 * RAD):
                xband[kx, i, y0 : y0 + RAD, :] = valid[2 + ky] * xband[kx, i, y0 : y0 + RAD, :]
        y0 = (BAND - RAD) * ky
        for i in range(nx - 2 * RAD):
            at = RAD * (RAD + i)
            inside = yband[ky, i, y0 : y0 + RAD, :] - message.rows(at, RAD)
            yband[ky, i, y0 : y0 + RAD, :] = valid[2 + ky] * inside

    stores = []
    for kx in range(2):
        for i in range(RAD):
            xout[kx, i] = xband[kx, RAD * (1 - kx) + i, RAD : RAD + ny, :].astype(jnp.bfloat16)
        stores.append(
            pltpu.make_async_copy(
                xout.at[kx], out_hbm.at[pl.ds((nx - RAD) * kx, RAD)], sems.at[kx]
            )
        )
    for ky in range(2):
        for i in range(nx - 2 * RAD):
            yout[ky, i] = yband[ky, i, RAD : RAD + SUB, :].astype(jnp.bfloat16)
        stores.append(
            pltpu.make_async_copy(
                yout.at[ky],
                out_hbm.at[pl.ds(RAD, nx - 2 * RAD), pl.ds((ny - SUB) * ky, SUB)],
                sems.at[2 + ky],
            )
        )
    for store in stores:
        store.start()
    for kx in range(2):
        for i in range(RAD):
            for j in range(ey // 8):
                rows = slice(8 * j, 8 * j + 8)
                pieces[(ex // 2 - RAD) * kx + i, 16 * j : 16 * j + 16, :] = packed(
                    xband[kx, 2 * i, rows, :], xband[kx, 2 * i + 1, rows, :]
                )
    for ky in range(2):
        rows = slice((BAND - 8) * ky, (BAND - 8) * ky + 8)
        at = 2 * (ey - 8) * ky
        for i in range(nx // 2 - RAD):
            pieces[RAD + i, at : at + 16, :] = packed(
                yband[ky, 2 * i, rows, :], yband[ky, 2 * i + 1, rows, :]
            )

    def edges(i, _):
        k = jnp.maximum(i - 2 * cols_n, 0)
        side = i < 2 * cols_n
        a = jnp.where(side, (i // cols_n) * (rows_n - 1), k // 2 + 1)
        b = jnp.where(side, i % cols_n, (k % 2) * (cols_n - 1))
        tile_gradient(own_atom(terms_ref, a * cols_n + b), grid, pieces, prof_x, grad_ref, a, b)
        return 0

    lax.fori_loop(0, 2 * cols_n + 2 * (rows_n - 2), edges, 0, unroll=10)
    for store in stores:
        store.wait()


def call(body, sizes, outs, in_specs, out_specs, scratch, cost, aliases=None):
    return pl.pallas_call(
        functools.partial(body, *sizes),
        out_shape=outs,
        in_specs=in_specs,
        out_specs=out_specs,
        scratch_shapes=scratch,
        input_output_aliases=aliases or {},
        cost_estimate=pl.CostEstimate(flops=cost, bytes_accessed=1 << 20, transcendentals=0),
        compiler_params=pltpu.CompilerParams(vmem_limit_bytes=VMEM_LIMIT),
    )


def local(atom_pos, b_factor, amplitude, counts, density_map):
    sizes = rows_n, cols_n = counts.shape
    nx, ny = rows_n * SUB, cols_n * SUB
    ex, ey = nx + 2 * RAD, ny + 2 * RAD
    f32, bf16 = jnp.float32, jnp.bfloat16
    shape = jax.ShapeDtypeStruct
    vmem = pl.BlockSpec(memory_space=pltpu.VMEM)
    hbm = pl.BlockSpec(memory_space=pltpu.HBM)
    pin = functools.partial(pltpu.with_memory_space_constraint, memory_space=pltpu.VMEM)
    own_scratch = [
        pltpu.SMEM(counts.shape, jnp.int32),
        pltpu.VMEM(atom_pos.shape, f32),
        pltpu.VMEM(b_factor.shape, f32),
        pltpu.VMEM(amplitude.shape, f32),
        pltpu.SemaphoreType.DMA((5,)),
    ]
    own = tuple(
        pltpu.with_memory_space_constraint(array, pltpu.HBM)
        for array in (counts, atom_pos, b_factor, amplitude)
    )
    density_map = pltpu.with_memory_space_constraint(density_map, pltpu.HBM)

    xsize, ysize = RAD * ny + FIELDS * cols_n, RAD * nx + BAND
    xlow, xhigh, first, second, found = call(
        message_kernel,
        sizes,
        (shape((xsize, CAP), f32),) * 2
        + (shape((ysize, CAP), f32),) * 2
        + (pltpu.VMEM((rows_n * cols_n, 8, CAP), f32),),
        [hbm] * 5,
        (vmem,) * 5,
        own_scratch
        + [
            pltpu.VMEM((2, RAD, ny, DEPTH), bf16),
            pltpu.VMEM((2, nx, 2 * RAD, DEPTH), bf16),
            pltpu.SemaphoreType.DMA((4,)),
        ],
        10**6,
    )(*own, density_map)
    from_first, from_second = swap(first, False), swap(second, True)
    from_xlow, from_xhigh = shift(xhigh, "bx", 1), shift(xlow, "bx", -1)

    bands = (
        pltpu.VMEM((2, 2 * RAD, ey, DEPTH), f32),
        pltpu.VMEM((2, nx - 2 * RAD, BAND, DEPTH), f32),
    )
    pieces = pltpu.VMEM((ex // 2, 2 * ey, 2 * DEPTH), bf16)
    residual, *kept, gradient = call(
        inner_kernel,
        sizes,
        (
            shape((nx, ny, DEPTH), bf16),
            pieces,
            *bands,
            shape((4, rows_n, cols_n, CAP), f32),
        ),
        [vmem, hbm],
        (hbm, vmem, vmem, vmem, vmem),
        [
            pltpu.VMEM((ex, ey, DEPTH), f32),
            pltpu.VMEM((nx, ny, DEPTH), bf16),
            pltpu.VMEM((nx, ny, DEPTH), bf16),
            pltpu.VMEM((3, TILE, CAP), f32),
            pltpu.SemaphoreType.DMA,
            pltpu.SemaphoreType.DMA((5,)),
        ],
        10**10,
    )(pin(found), density_map)
    kept_pieces, xband, yband = kept

    edge = shape((2 * (RAD * RAD + FIELDS) + 6, CAP), f32)
    up, down = call(
        corner_kernel, sizes, (edge, edge), [vmem, vmem], (vmem, vmem), [], 10**5
    )(from_first, from_second)
    from_corners = shift(up, "bx", 1), shift(down, "bx", -1)

    messages = (from_xlow, from_xhigh, from_first, from_second)
    xband, yband = call(
        sides_kernel,
        sizes,
        bands,
        [vmem] * 6,
        (vmem, vmem),
        [],
        2 * 10**9,
        {4: 0, 5: 1},
    )(*messages, pin(xband), pin(yband))

    residual, gradient, *_ = call(
        outer_kernel,
        sizes,
        (
            shape((nx, ny, DEPTH), bf16),
            shape((4, rows_n, cols_n, CAP), f32),
            *bands,
            pieces,
        ),
        [vmem] * 11 + [hbm],
        (hbm, vmem, vmem, vmem, vmem),
        [
            pltpu.VMEM((2, RAD, ny, DEPTH), bf16),
            pltpu.VMEM((2, nx - 2 * RAD, SUB, DEPTH), bf16),
            pltpu.VMEM((3, TILE, CAP), f32),
            pltpu.SemaphoreType.DMA((4,)),
        ],
        10**10,
        {11: 0, 7: 2, 8: 3, 9: 4},
    )(
        pin(found), *messages, *from_corners,
        pin(xband), pin(yband), pin(kept_pieces), gradient, residual,
    )
    return residual, gradient


def solution(mesh):
    return jax.shard_map(
        local,
        mesh=mesh,
        in_specs=(
            P(None, "bx", "by", None),
            P("bx", "by", None),
            P("bx", "by", None),
            P("bx", "by"),
            P("bx", "by", None),
        ),
        out_specs=(P("bx", "by", None), P(None, "bx", "by", None)),
        check_vma=False,
    )
```

```python
import functools
import math

import jax
import jax.numpy as jnp
from jax import lax
from jax.experimental import pallas as pl
from jax.experimental.pallas import tpu as pltpu
from jax.sharding import PartitionSpec as P

SUB = 16
RAD = 4
TILE = 24
CAP = 128
DEPTH = 128
FIELDS = 5
BAND = 24

EIGHT_PI_SQ = 8.0 * math.pi**2
BLUR_VAR = 0.5
REACH_SQ = float(RAD * RAD)
LOG2_E = math.log2(math.e)
VMEM_LIMIT = 18 << 20


def shift(block, axis, step):
    peers = lax.axis_size(axis)
    route = [(i, (i + step) % peers) for i in range(peers)]
    return lax.ppermute(block, axis, route)


def swap(block, odd):
    nx, ny = lax.axis_size("bx"), lax.axis_size("by")
    route = []
    for x in range(nx):
        for y in range(ny):
            to_x, to_y = x, (y ^ 1 if not odd else ((y + 1) ^ 1) - 1)
            if not 0 <= to_y < ny:
                to_x, to_y = x ^ 1, y
            route.append((x * ny + y, to_x * ny + to_y))
    return lax.ppermute(block, ("bx", "by"), route)


def is_even():
    return lax.axis_index("by") % 2 == 0


def valid_sides():
    found = []
    for axis in ("bx", "by"):
        at = lax.axis_index(axis)
        found += [at > 0, at < lax.axis_size(axis) - 1]
    return [jnp.where(side, 1.0, 0.0) for side in found]


class Picked:
    def __init__(self, flag, when_true, when_false):
        self.flag, self.refs = flag, (when_true, when_false)

    def rows(self, at, count):
        where = pl.ds(at, count)
        return jnp.where(self.flag, self.refs[0][where, :], self.refs[1][where, :])


class Plain:
    def __init__(self, ref):
        self.ref = ref

    def rows(self, at, count):
        return self.ref[pl.ds(at, count), :]


def split(value):
    high = value.astype(jnp.bfloat16)
    low = (value - high.astype(jnp.float32)).astype(jnp.bfloat16)
    return high, low


def grid_of(span):
    return lax.broadcasted_iota(jnp.int32, (span, CAP), 0).astype(jnp.float32)


def base_profile(coordinate, sharpness, grid):
    distance = grid - coordinate
    square = distance * distance
    falloff = jnp.maximum(1.0 - square * (1.0 / REACH_SQ), 0.0)
    damped = jnp.exp2(square * (sharpness * (-LOG2_E))) * falloff
    return distance, square, falloff, damped


def value_only(coordinate, sharpness, grid):
    _, _, falloff, damped = base_profile(coordinate, sharpness, grid)
    return damped * falloff


def all_kinds(coordinate, sharpness, grid):
    distance, square, falloff, damped = base_profile(coordinate, sharpness, grid)
    value = damped * falloff
    slope = distance * (2.0 * sharpness * value + (4.0 / REACH_SQ) * damped)
    width = -square * value
    return value, slope, width


def terms(x, y, z, b_factor):
    cx, cy, cz = x * float(SUB), y * float(SUB), z * float(DEPTH)
    return cx, cy, cz, 0.5 / (b_factor / EIGHT_PI_SQ + BLUR_VAR)


def fetch(pairs, sems):
    copies = [pltpu.make_async_copy(a, b, sems.at[i]) for i, (a, b) in enumerate(pairs)]
    for copy in copies:
        copy.start()
    return copies


def finish(copies):
    for copy in copies:
        copy.wait()


def masked(amplitude, count):
    slot = lax.broadcasted_iota(jnp.int32, (1, CAP), 1)
    return jnp.where(slot < count, amplitude, 0.0)


def own_atom(terms_ref, index):
    return tuple(terms_ref[index, k : k + 1, :] for k in range(FIELDS))


def sent_atom(message, start, stride, index, valid):
    row = [message.rows(start + k * stride + index, 1) for k in range(FIELDS)]
    return terms(*row[:4]) + (row[4] * valid,)


def rendered(atom, z_parts, p0, p_n, j0, j_n):
    cx, cy, cz, sharp, weight = atom
    grid = grid_of(TILE) - float(RAD)
    vx = value_only(cx, sharp, grid[p0 : p0 + p_n]) * weight
    vy = value_only(cy, sharp, grid[8 * j0 : 8 * j0 + 8 * j_n])
    z_hi, z_lo = z_parts
    weights = jnp.concatenate(
        [jnp.concatenate([z_hi, z_hi], 1), jnp.concatenate([z_lo, z_lo], 1)], 0
    )
    out = []
    step = TILE // 2 if p_n == TILE else p_n
    for start in range(0, p_n, step):
        rows = []
        for p in range(start, start + step):
            for j in range(j_n):
                rows.append(vx[p : p + 1] * vy[8 * j : 8 * j + 8])
        plane_hi, plane_lo = split(jnp.concatenate(rows, 0))
        plane = jnp.concatenate([plane_hi, plane_lo], 1)
        both = lax.dot_general(
            plane, weights, (((1,), (1,)), ((), ())), preferred_element_type=jnp.float32
        )
        total = both[:, :DEPTH] + both[:, DEPTH:]
        out += [total[8 * j_n * p : 8 * j_n * (p + 1)] for p in range(step)]
    return out


def z_value(atom, grid):
    return split(value_only(atom[2], atom[3], grid))


def packed(first, second):
    hi, lo = split(jnp.concatenate([first, second], 0))
    return jnp.concatenate([hi, lo], 1)


def tile_gradient(atom, z_grid, pieces, prof_x, grad_ref, a, b):
    cx, cy, cz, sharp, weight = atom
    grid = grid_of(TILE) - float(RAD)
    for k, kind in enumerate(all_kinds(cx, sharp, grid)):
        prof_x[k] = kind
    vy, sy, wy = all_kinds(cy, sharp, grid)
    vz, sz, wz = all_kinds(cz, sharp, z_grid)
    vz_hi, vz_lo = split(vz)
    sz_hi, sz_lo = split(sz)
    wz_hi = wz.astype(jnp.bfloat16)
    tile = pieces[pl.ds(8 * a, TILE // 2), pl.ds(pl.multiple_of(32 * b, 32), 2 * TILE), :]
    tile = tile.reshape(TILE * TILE, 2 * DEPTH)

    def project(rhs):
        return jnp.dot(tile, jnp.concatenate([rhs, rhs], 0), preferred_element_type=jnp.float32)

    proj_v = project(jnp.concatenate([vz_hi, vz_lo], 1))
    proj_s = project(jnp.concatenate([sz_hi, sz_lo], 1))
    proj_w = project(wz_hi)
    acc = [[jnp.zeros((8, CAP), jnp.float32) for _ in range(3)] for _ in range(4)]
    for p in range(TILE):
        vx = prof_x[0, p : p + 1, :]
        sx = prof_x[1, p : p + 1, :]
        wx = prof_x[2, p : p + 1, :]
        for j in range(3):
            at = ((p // 2) * 3 + j) * 16 + (p % 2) * 8
            base = proj_v[at : at + 8, :CAP] + proj_v[at : at + 8, CAP:]
            lift = proj_s[at : at + 8, :CAP] + proj_s[at : at + 8, CAP:]
            wide = proj_w[at : at + 8]
            acc[0][j] += base * vx
            acc[1][j] += base * sx
            acc[2][j] += lift * vx
            acc[3][j] += base * wx + wide * vx
    g_x = g_y = g_z = g_s = 0.0
    for j in range(3):
        at = slice(8 * j, 8 * j + 8)
        g_x += acc[1][j] * vy[at]
        g_y += acc[0][j] * sy[at]
        g_z += acc[2][j] * vy[at]
        g_s += acc[3][j] * vy[at] + acc[0][j] * wy[at]
    scale = -2.0 * sharp * sharp / EIGHT_PI_SQ
    for k, g in enumerate((g_x, g_y, g_z, g_s)):
        g = weight * jnp.sum(g, axis=0, keepdims=True)
        if k == 3:
            g = g * scale
        grad_ref[k, a, pl.ds(b, 1), :] = g


def message_kernel(
    rows_n, cols_n,
    counts_hbm, pos_hbm, bfac_hbm, amp_hbm, map_hbm,
    xlow_ref, xhigh_ref, first_ref, second_ref, terms_ref,
    counts_ref, pos_ref, bfac_ref, amp_ref, own_sems,
    xrim, yrim, sems,
):
    nx, ny = rows_n * SUB, cols_n * SUB
    held = (counts_ref, pos_ref, bfac_ref, amp_ref)
    fetched = fetch(zip((counts_hbm, pos_hbm, bfac_hbm, amp_hbm), held), own_sems)
    copies = []
    for k, at in enumerate((0, nx - RAD)):
        copies.append(pltpu.make_async_copy(map_hbm.at[pl.ds(at, RAD)], xrim.at[k], sems.at[k]))
    for k, at in enumerate((0, ny - 2 * RAD)):
        copies.append(
            pltpu.make_async_copy(map_hbm.at[:, pl.ds(at, 2 * RAD)], yrim.at[k], sems.at[2 + k])
        )
    for copy in copies:
        copy.start()

    def fields(a, b):
        found = [pos_ref[k, a, b : b + 1, :] for k in range(3)] + [bfac_ref[a, b : b + 1, :]]
        return found + [masked(amp_ref[a, b : b + 1, :], counts_ref[a, b])]

    def atoms(out, start, stride, index, a, b):
        for k, value in enumerate(fields(a, b)):
            out[start + k * stride + index : start + k * stride + index + 1, :] = value

    finish(fetched)
    for a in range(rows_n):
        found = terms(pos_ref[0, a], pos_ref[1, a], pos_ref[2, a], bfac_ref[a])
        for b in range(cols_n):
            row = slice(b, b + 1)
            weight = masked(amp_ref[a, row, :], counts_ref[a, b])
            terms_ref[a * cols_n + b, 0:FIELDS, :] = jnp.concatenate(
                [value[row] for value in found] + [weight], 0
            )
    for b in range(cols_n):
        atoms(xlow_ref, RAD * ny, cols_n, b, 0, b)
        atoms(xhigh_ref, RAD * ny, cols_n, b, rows_n - 1, b)
    even = is_even()

    def put(where, low, high):
        first_ref[where, :] = jnp.where(even, high, low)
        second_ref[where, :] = jnp.where(even, low, high)

    for out in (first_ref, second_ref):
        out[nx * RAD :, :] = jnp.zeros((BAND, CAP), jnp.float32)
    for a in range(rows_n):
        low, high = fields(a, 0), fields(a, cols_n - 1)
        for k in range(FIELDS):
            at = RAD * nx + k * rows_n + a
            put(slice(at, at + 1), low[k], high[k])
    for copy in copies:
        copy.wait()
    for k, out in enumerate((xlow_ref, xhigh_ref)):
        for i in range(RAD):
            out[ny * i : ny * (i + 1), :] = xrim[k, i].astype(jnp.float32)
    for i in range(nx):
        put(
            slice(RAD * i, RAD * (i + 1)),
            yrim[0, i].astype(jnp.float32)[:RAD],
            yrim[1, i].astype(jnp.float32)[RAD:],
        )


def inner_kernel(
    rows_n, cols_n,
    terms_ref, map_hbm,
    out_hbm, pieces, xband, yband, grad_ref,
    field, map_v, out_v, prof_x, in_sem, out_sems,
):
    nx, ny = rows_n * SUB, cols_n * SUB
    ex, ey = nx + 2 * RAD, ny + 2 * RAD
    load = pltpu.make_async_copy(map_hbm, map_v, in_sem)
    load.start()

    for i in range(2 * RAD):
        field[i] = jnp.zeros((ey, DEPTH), jnp.float32)
    for i in range(2 * RAD, ex):
        field[i, 0 : 2 * RAD, :] = jnp.zeros((2 * RAD, DEPTH), jnp.float32)

    grid = grid_of(DEPTH)

    def own(i, _):
        a, b = i // cols_n, i % cols_n
        y0 = pl.multiple_of(SUB * b, SUB)
        y1 = pl.multiple_of(SUB * b + 2 * RAD, 2 * RAD)
        atom = own_atom(terms_ref, i)
        for p, row in enumerate(rendered(atom, z_value(atom, grid), 0, TILE, 0, 3)):
            if p < 2 * RAD:
                field[SUB * a + p, pl.ds(y0, TILE), :] += row
            else:
                field[SUB * a + p, pl.ds(y0, 2 * RAD), :] += row[: 2 * RAD]
                field[SUB * a + p, pl.ds(y1, SUB), :] = row[2 * RAD :]
        return 0

    lax.fori_loop(0, rows_n * cols_n, own, 0, unroll=16)
    load.wait()

    def brick(i, _):
        inside = field[i + RAD, RAD : RAD + ny, :] - map_v[i].astype(jnp.float32)
        field[i + RAD, RAD : RAD + ny, :] = inside
        out_v[i] = inside.astype(jnp.bfloat16)
        return 0

    lax.fori_loop(0, nx, brick, 0, unroll=8)
    rest = pl.ds(2 * RAD, nx - 2 * RAD)
    pairs = [(out_v, out_hbm)]
    for k in range(2):
        pairs.append((field.at[pl.ds((ex - 2 * RAD) * k, 2 * RAD)], xband.at[k]))
        pairs.append((field.at[rest, pl.ds((ey - BAND) * k, BAND)], yband.at[k]))
    stores = fetch(pairs, out_sems)

    def pack(i, _):
        for j in range(ey // 8):
            rows = pl.ds(8 * j, 8)
            pieces[i, 16 * j : 16 * j + 16, :] = packed(field[2 * i, rows, :], field[2 * i + 1, rows, :])
        return 0

    lax.fori_loop(RAD, ex // 2 - RAD, pack, 0, unroll=4)
    def gradient(i, _):
        a, b = i // (cols_n - 2) + 1, i % (cols_n - 2) + 1
        tile_gradient(own_atom(terms_ref, a * cols_n + b), grid, pieces, prof_x, grad_ref, a, b)
        return 0

    lax.fori_loop(0, (rows_n - 2) * (cols_n - 2), gradient, 0, unroll=12)
    finish(stores)


def corner_kernel(rows_n, cols_n, first_ref, second_ref, up_ref, down_ref):
    nx = rows_n * SUB
    even = is_even()
    ylow, yhigh = Picked(even, second_ref, first_ref), Picked(even, first_ref, second_ref)
    block = RAD * RAD
    for out, x0, a in ((up_ref, nx - RAD, rows_n - 1), (down_ref, 0, 0)):
        for ky, message in enumerate((ylow, yhigh)):
            at = (block + FIELDS) * ky
            out[at : at + block, :] = message.rows(RAD * x0, block)
            for k in range(FIELDS):
                row = at + block + k
                out[row : row + 1, :] = message.rows(RAD * nx + k * rows_n + a, 1)
        at = 2 * (block + FIELDS)
        out[at:, :] = jnp.zeros((out.shape[0] - at, CAP), jnp.float32)


def sides_kernel(
    rows_n, cols_n,
    xlow_ref, xhigh_ref, first_ref, second_ref, xband_in, yband_in,
    xband, yband,
):
    nx, ny = rows_n * SUB, cols_n * SUB
    ex, ey = nx + 2 * RAD, ny + 2 * RAD
    even, valid = is_even(), valid_sides()
    ylow, yhigh = Picked(even, second_ref, first_ref), Picked(even, first_ref, second_ref)
    grid = grid_of(DEPTH)

    def x_side(b, _):
        y0 = pl.multiple_of(SUB * b, SUB)
        for k, (message, p0) in enumerate(((Plain(xlow_ref), SUB), (Plain(xhigh_ref), 0))):
            atom = sent_atom(message, RAD * ny, cols_n, b, valid[k])
            for p, row in enumerate(rendered(atom, z_value(atom, grid), p0, 2 * RAD, 0, 3)):
                xband[k, p, pl.ds(y0, TILE), :] += row
        return 0

    lax.fori_loop(0, cols_n, x_side, 0, unroll=8)
    for a in range(rows_n):
        for k, (message, j0, y0) in enumerate(((ylow, 2, 0), (yhigh, 0, ey - 8))):
            atom = sent_atom(message, RAD * nx, rows_n, a, valid[2 + k])
            for p, row in enumerate(rendered(atom, z_value(atom, grid), 0, TILE, j0, 1)):
                x = SUB * a + p
                if x < 2 * RAD:
                    xband[0, x, y0 : y0 + 8, :] += row
                elif x >= ex - 2 * RAD:
                    xband[1, x - (ex - 2 * RAD), y0 : y0 + 8, :] += row
                else:
                    yband[k, x - 2 * RAD, (BAND - 8) * k : (BAND - 8) * k + 8, :] += row


def outer_kernel(
    rows_n, cols_n,
    terms_ref, xlow_ref, xhigh_ref, first_ref, second_ref, clow_ref, chigh_ref,
    xband_in, yband_in, pieces_in, grad_in, out_in,
    out_hbm, grad_ref, xband, yband, pieces,
    xout, yout, prof_x, sems,
):
    nx, ny = rows_n * SUB, cols_n * SUB
    ex, ey = nx + 2 * RAD, ny + 2 * RAD
    grad_ref[...] = grad_in[...]
    corner = RAD * RAD + FIELDS
    even, valid = is_even(), valid_sides()
    ylow, yhigh = Picked(even, second_ref, first_ref), Picked(even, first_ref, second_ref)
    sent = Plain(clow_ref), Plain(chigh_ref)
    grid = grid_of(DEPTH)
    for ky, (j0, y0) in enumerate(((2, 0), (0, ey - 8))):
        for kx, p0 in enumerate((SUB, 0)):
            ok = valid[kx] * valid[2 + ky]
            atom = sent_atom(sent[kx], corner * ky + RAD * RAD, 1, 0, ok)
            for p, row in enumerate(rendered(atom, z_value(atom, grid), p0, 2 * RAD, j0, 1)):
                xband[kx, p, y0 : y0 + 8, :] += row
    for kx, message in enumerate((xlow_ref, xhigh_ref)):
        for i in range(RAD):
            row = RAD * kx + i
            xband[kx, row, RAD : RAD + ny, :] -= message[ny * i : ny * (i + 1), :]
            for ky in range(2):
                y0 = (ey - RAD) * ky
                xband[kx, row, y0 : y0 + RAD, :] -= sent[kx].rows(corner * ky + RAD * i, RAD)
            xband[kx, row] = valid[kx] * xband[kx, row]
    for ky, message in enumerate((ylow, yhigh)):
        y0 = (ey - RAD) * ky
        for kx in range(2):
            for i in range(RAD):
                row = RAD * (1 - kx) + i
                at = RAD * ((nx - RAD) * kx + i)
                xband[kx, row, y0 : y0 + RAD, :] -= message.rows(at, RAD)
            for i in range(2 * RAD):
                xband[kx, i, y0 : y0 + RAD, :] = valid[2 + ky] * xband[kx, i, y0 : y0 + RAD, :]
        y0 = (BAND - RAD) * ky
        for i in range(nx - 2 * RAD):
            at = RAD * (RAD + i)
            inside = yband[ky, i, y0 : y0 + RAD, :] - message.rows(at, RAD)
            yband[ky, i, y0 : y0 + RAD, :] = valid[2 + ky] * inside

    stores = []
    for kx in range(2):
        for i in range(RAD):
            xout[kx, i] = xband[kx, RAD * (1 - kx) + i, RAD : RAD + ny, :].astype(jnp.bfloat16)
        stores.append(
            pltpu.make_async_copy(
                xout.at[kx], out_hbm.at[pl.ds((nx - RAD) * kx, RAD)], sems.at[kx]
            )
        )
    for ky in range(2):
        for i in range(nx - 2 * RAD):
            yout[ky, i] = yband[ky, i, RAD : RAD + SUB, :].astype(jnp.bfloat16)
        stores.append(
            pltpu.make_async_copy(
                yout.at[ky],
                out_hbm.at[pl.ds(RAD, nx - 2 * RAD), pl.ds((ny - SUB) * ky, SUB)],
                sems.at[2 + ky],
            )
        )
    for store in stores:
        store.start()
    for kx in range(2):
        for i in range(RAD):
            for j in range(ey // 8):
                rows = slice(8 * j, 8 * j + 8)
                pieces[(ex // 2 - RAD) * kx + i, 16 * j : 16 * j + 16, :] = packed(
                    xband[kx, 2 * i, rows, :], xband[kx, 2 * i + 1, rows, :]
                )
    for ky in range(2):
        rows = slice((BAND - 8) * ky, (BAND - 8) * ky + 8)
        at = 2 * (ey - 8) * ky
        for i in range(nx // 2 - RAD):
            pieces[RAD + i, at : at + 16, :] = packed(
                yband[ky, 2 * i, rows, :], yband[ky, 2 * i + 1, rows, :]
            )

    def edges(i, _):
        k = jnp.maximum(i - 2 * cols_n, 0)
        side = i < 2 * cols_n
        a = jnp.where(side, (i // cols_n) * (rows_n - 1), k // 2 + 1)
        b = jnp.where(side, i % cols_n, (k % 2) * (cols_n - 1))
        tile_gradient(own_atom(terms_ref, a * cols_n + b), grid, pieces, prof_x, grad_ref, a, b)
        return 0

    lax.fori_loop(0, 2 * cols_n + 2 * (rows_n - 2), edges, 0, unroll=10)
    for store in stores:
        store.wait()


def call(body, sizes, outs, in_specs, out_specs, scratch, cost, aliases=None):
    return pl.pallas_call(
        functools.partial(body, *sizes),
        out_shape=outs,
        in_specs=in_specs,
        out_specs=out_specs,
        scratch_shapes=scratch,
        input_output_aliases=aliases or {},
        cost_estimate=pl.CostEstimate(flops=cost, bytes_accessed=1 << 20, transcendentals=0),
        compiler_params=pltpu.CompilerParams(vmem_limit_bytes=VMEM_LIMIT),
    )


def local(atom_pos, b_factor, amplitude, counts, density_map):
    sizes = rows_n, cols_n = counts.shape
    nx, ny = rows_n * SUB, cols_n * SUB
    ex, ey = nx + 2 * RAD, ny + 2 * RAD
    f32, bf16 = jnp.float32, jnp.bfloat16
    shape = jax.ShapeDtypeStruct
    vmem = pl.BlockSpec(memory_space=pltpu.VMEM)
    hbm = pl.BlockSpec(memory_space=pltpu.HBM)
    pin = functools.partial(pltpu.with_memory_space_constraint, memory_space=pltpu.VMEM)
    own_scratch = [
        pltpu.SMEM(counts.shape, jnp.int32),
        pltpu.VMEM(atom_pos.shape, f32),
        pltpu.VMEM(b_factor.shape, f32),
        pltpu.VMEM(amplitude.shape, f32),
        pltpu.SemaphoreType.DMA((5,)),
    ]
    own = tuple(
        pltpu.with_memory_space_constraint(array, pltpu.HBM)
        for array in (counts, atom_pos, b_factor, amplitude)
    )
    density_map = pltpu.with_memory_space_constraint(density_map, pltpu.HBM)

    xsize, ysize = RAD * ny + FIELDS * cols_n, RAD * nx + BAND
    xlow, xhigh, first, second, found = call(
        message_kernel,
        sizes,
        (shape((xsize, CAP), f32),) * 2
        + (shape((ysize, CAP), f32),) * 2
        + (pltpu.VMEM((rows_n * cols_n, 8, CAP), f32),),
        [hbm] * 5,
        (vmem,) * 5,
        own_scratch
        + [
            pltpu.VMEM((2, RAD, ny, DEPTH), bf16),
            pltpu.VMEM((2, nx, 2 * RAD, DEPTH), bf16),
            pltpu.SemaphoreType.DMA((4,)),
        ],
        10**6,
    )(*own, density_map)
    from_first, from_second = swap(first, False), swap(second, True)
    from_xlow, from_xhigh = shift(xhigh, "bx", 1), shift(xlow, "bx", -1)

    bands = (
        pltpu.VMEM((2, 2 * RAD, ey, DEPTH), f32),
        pltpu.VMEM((2, nx - 2 * RAD, BAND, DEPTH), f32),
    )
    pieces = pltpu.VMEM((ex // 2, 2 * ey, 2 * DEPTH), bf16)
    residual, *kept, gradient = call(
        inner_kernel,
        sizes,
        (
            shape((nx, ny, DEPTH), bf16),
            pieces,
            *bands,
            shape((4, rows_n, cols_n, CAP), f32),
        ),
        [vmem, hbm],
        (hbm, vmem, vmem, vmem, vmem),
        [
            pltpu.VMEM((ex, ey, DEPTH), f32),
            pltpu.VMEM((nx, ny, DEPTH), bf16),
            pltpu.VMEM((nx, ny, DEPTH), bf16),
            pltpu.VMEM((3, TILE, CAP), f32),
            pltpu.SemaphoreType.DMA,
            pltpu.SemaphoreType.DMA((5,)),
        ],
        10**10,
    )(pin(found), density_map)
    kept_pieces, xband, yband = kept

    edge = shape((2 * (RAD * RAD + FIELDS) + 6, CAP), f32)
    up, down = call(
        corner_kernel, sizes, (edge, edge), [vmem, vmem], (vmem, vmem), [], 10**5
    )(from_first, from_second)
    from_corners = shift(up, "bx", 1), shift(down, "bx", -1)

    messages = (from_xlow, from_xhigh, from_first, from_second)
    xband, yband = call(
        sides_kernel,
        sizes,
        bands,
        [vmem] * 6,
        (vmem, vmem),
        [],
        2 * 10**9,
        {4: 0, 5: 1},
    )(*messages, pin(xband), pin(yband))

    residual, gradient, *_ = call(
        outer_kernel,
        sizes,
        (
            shape((nx, ny, DEPTH), bf16),
            shape((4, rows_n, cols_n, CAP), f32),
            *bands,
            pieces,
        ),
        [vmem] * 11 + [hbm],
        (hbm, vmem, vmem, vmem, vmem),
        [
            pltpu.VMEM((2, RAD, ny, DEPTH), bf16),
            pltpu.VMEM((2, nx - 2 * RAD, SUB, DEPTH), bf16),
            pltpu.VMEM((3, TILE, CAP), f32),
            pltpu.SemaphoreType.DMA((4,)),
        ],
        10**10,
        {11: 0, 7: 2, 8: 3, 9: 4},
    )(
        pin(found), *messages, *from_corners,
        pin(xband), pin(yband), pin(kept_pieces), gradient, residual,
    )
    return residual, gradient


def solution(mesh):
    return jax.shard_map(
        local,
        mesh=mesh,
        in_specs=(
            P(None, "bx", "by", None),
            P("bx", "by", None),
            P("bx", "by", None),
            P("bx", "by"),
            P("bx", "by", None),
        ),
        out_specs=(P("bx", "by", None), P(None, "bx", "by", None)),
        check_vma=False,
    )
```
